32 devices in a mesh: dp: 4 (over x, core), expert: 8 (over z, y).
Axes of the slice: x: 2, y: 2, z: 4, core: 2. Of those that a mesh axis runs over, the one named last changes fastest.
Arguments:
- tokens: bfloat16 [4096, 2048], P(('dp', 'expert')), may hold values from -6 to 6
- expert_ids: int32 [4096, 4], P(('dp', 'expert')), may hold values from 0 to 15, all different within a row; in each aligned block of 128 rows (0 to 127, 128 to 255, ...) at most 48 rows name the same one
- gate_weights: float32 [4096, 4], P(('dp', 'expert')), may hold values from 0.05 to 0.6
- grad_out: bfloat16 [4096, 2048], P(('dp', 'expert')), may hold values from -6 to 6
- w_gate: bfloat16 [16, 2048, 384], P('expert'), may hold values from -0.125 to 0.125
- w_up: bfloat16 [16, 2048, 384], P('expert'), may hold values from -0.125 to 0.125
- w_down: bfloat16 [16, 384, 2048], P('expert'), may hold values from -0.3125 to 0.3125
Outputs:
- mixed_out: bfloat16 [4096, 2048], P(('dp', 'expert'))
- d_tokens: bfloat16 [4096, 2048], P(('dp', 'expert'))
- d_gates: float32 [4096, 4], P(('dp', 'expert'))
- d_w_gate: bfloat16 [16, 2048, 384], P('expert', 'dp')
- d_w_up: bfloat16 [16, 2048, 384], P('expert', 'dp')
- d_w_down: bfloat16 [16, 384, 2048], P('expert', None, 'dp')
The draws below stay inside these ranges and needn't reach their ends.
Inputs may be any that keep to these rules, and one draw needn't show every extreme that they name: `expert_ids`: each row names 4 different experts; in the 128 rows of one device no expert is named more than 48 times, and in every draw some expert is named exactly 48 times by the rows of some device.
All inputs are finite; a program needn't handle non-finite values.
Results may differ from the reference program's by a relative error of at most 0.009.
Values may be sent and summed in bfloat16 or wider, within the bound.
A program may use at most 128 MiB of HBM per device.

```python
import math
import jax
import jax.numpy as jnp
import numpy as np
from jax import lax

D = 2048
FF = 384
TOP = 4
TOK_DEV = 128
EXPERTS = 16
CAP = 48
TOKENS = 4096
N_DP = 4
N_EXPERT = 8


def shard_levels(stream_key, shape, pieces, low, top_value):
    def one(dim, shards_of):
        draws = jax.random.uniform(jax.random.fold_in(jax.random.fold_in(stream_key, 6), dim), (shards_of,), jnp.float32, low / len(pieces), top_value / len(pieces))
        return jnp.repeat(jnp.exp(draws), shape[dim] // shards_of).reshape((-1,) + (1,) * (len(shape) - dim - 1))

    factor_of = one(*pieces[0])
    for cut in pieces[1:]:
        factor_of = factor_of * one(*cut)
    return factor_of


def deal_out(rng, own, number, rows, number_of, top, limit, skew):
    order = jax.random.permutation(rng, number_of)
    packed, usual = shares(number_of, rows * top, limit, skew, True), shares(number_of, rows * top, limit, skew, False)
    places = jnp.arange(number_of)

    def named(tallies, rotation):
        used = int((tallies > 0).sum())
        fixed = max(1, used // 4)
        shifted = fixed + (places - fixed + rotation * (used - fixed)) % max(1, number_of - fixed)
        return jnp.zeros((number_of,), jnp.int32).at[order[jnp.where(places < fixed, places, shifted)]].set(jnp.asarray(tallies, jnp.int32))

    tallies = jnp.where(number % 4 == 0, named(packed, number // 4), named(usual, number - number // 4 - 1))
    mixed = jax.random.permutation(jax.random.fold_in(own, 3), number_of)
    donor, taker = mixed[0:number_of // 2 * 2:2], mixed[1:number_of // 2 * 2:2]
    slack = jnp.minimum(tallies[donor] - 1, limit - tallies[taker]) // 2
    slack = jnp.where((donor == order[0]) | (taker == order[0]) | (tallies[taker] == 0), 0, jnp.maximum(slack, 0))
    shifted = jax.random.randint(jax.random.fold_in(own, 4), (number_of // 2,), 0, 1 << 20) % (slack + 1)
    tallies = tallies.at[donor].add(-shifted).at[taker].add(shifted)
    members = jnp.searchsorted(jnp.cumsum(tallies), jnp.arange(rows * top), side="right").astype(jnp.int32)
    grid = members.reshape(top, rows).T
    grid = grid[jax.random.permutation(jax.random.fold_in(own, 1), rows)]
    rotation = jax.random.randint(jax.random.fold_in(own, 2), (rows, 1), 0, top)
    return jnp.take_along_axis(grid, (jnp.arange(top)[None, :] + rotation) % top, axis=1)


def shares(number_of, total, most, skew, full):
    weights = [(1 << 20) // math.isqrt(rank ** skew) + 1 for rank in range(1, number_of + 1)]
    largest = most if full else min(most, max(-(-total // number_of), total * weights[0] // sum(weights)))
    least = 1 if total - largest >= number_of - 1 else 0
    holding, rest = [largest] + [least] * (number_of - 1), total - largest - least * (number_of - 1)
    while rest > 0:
        free = [i for i in range(1, number_of) if holding[i] < largest] or [i for i in range(1, number_of) if holding[i] < most]
        mass, budget = sum([weights[i] for i in free]), rest
        for i in free:
            extra = min(most - holding[i], max(1, budget * weights[i] // mass), rest)
            holding[i] = holding[i] + extra
            rest = rest - extra
    return np.array(holding)


def gaussian(rng, extent, deviation, reach, pieces=(), held_as=jnp.bfloat16):
    entries = deviation * jax.random.normal(rng, extent, jnp.float32)
    if pieces:
        entries = entries * shard_levels(rng, extent, pieces, -0.22, 0.18)
    return jnp.clip(entries, -reach, reach).astype(held_as)


def setup_inputs(seed: int = 0) -> dict:
    arg_keys = jax.random.split(jax.random.key(seed), 8)
    tokens = gaussian(arg_keys[0], (TOKENS, D), 1.0, 6.0, ((0, 32),))
    expert_ids_keys = jax.random.split(jax.random.fold_in(arg_keys[1], 1), TOKENS // TOK_DEV)
    expert_ids_turns = jax.random.permutation(jax.random.fold_in(arg_keys[1], 3), TOKENS // TOK_DEV)
    expert_ids = jax.vmap(lambda own, number: deal_out(jax.random.fold_in(arg_keys[1], 2), own, number, TOK_DEV, EXPERTS, TOP, CAP, 2))(expert_ids_keys, expert_ids_turns).reshape((TOKENS, TOP))
    gate_weights = jnp.clip(0.05 + 0.55 * jax.random.uniform(arg_keys[2], (TOKENS, TOP), jnp.float32) ** shard_levels(arg_keys[2], (TOKENS, TOP), ((0, 32),), -0.2, 0.2), 0.05, 0.6)
    grad_out = gaussian(arg_keys[3], (TOKENS, D), 1.0, 6.0, ((0, 32),))
    w_gate = gaussian(arg_keys[4], (EXPERTS, D, FF), D ** -0.5, 0.125, ((0, 8),))
    w_up = gaussian(arg_keys[5], (EXPERTS, D, FF), D ** -0.5, 0.125, ((0, 8),))
    w_down = gaussian(arg_keys[6], (EXPERTS, FF, D), FF ** -0.5, 0.3125, ((0, 8),))
    return dict(tokens=tokens, expert_ids=expert_ids, gate_weights=gate_weights, grad_out=grad_out, w_gate=w_gate, w_up=w_up, w_down=w_down)


def summed_groups(partials):
    rounded = partials.astype(jnp.bfloat16)
    rounded = lax.optimization_barrier(rounded)
    return jnp.sum(rounded.astype(jnp.float32), axis=0).astype(jnp.bfloat16)


def reference(tokens, expert_ids, gate_weights, grad_out, w_gate, w_up, w_down):
    device_count = N_DP * N_EXPERT
    routes_dev = TOK_DEV * TOP
    slot_count = device_count * CAP
    route_total = TOKENS * TOP
    ids_dev = expert_ids.reshape(device_count, routes_dev).astype(jnp.int32)
    onehot = (ids_dev[:, :, None] == jnp.arange(EXPERTS, dtype=jnp.int32)[None, None, :]).astype(jnp.int32)
    earlier = jnp.cumsum(onehot, axis=1) - onehot
    slot_pos = jnp.sum(earlier * onehot, axis=2).astype(jnp.int32)
    device_ids = jnp.arange(device_count, dtype=jnp.int32)[:, None]
    position = (ids_dev * slot_count + device_ids * CAP + slot_pos).reshape(-1).astype(jnp.int32)
    route_of = jnp.full((EXPERTS * slot_count,), route_total, dtype=jnp.int32)
    route_of = route_of.at[position].set(jnp.arange(route_total, dtype=jnp.int32)).reshape(EXPERTS, slot_count)
    tokens_ext = jnp.concatenate([tokens, jnp.zeros((1, D), tokens.dtype)], axis=0)
    grad_ext = jnp.concatenate([grad_out, jnp.zeros((1, D), grad_out.dtype)], axis=0)
    gates_ext = jnp.concatenate([gate_weights.reshape(-1), jnp.zeros((1,), gate_weights.dtype)], axis=0)

    def per_expert(totals, inputs):
        out_acc, dx_acc, dgate_acc = totals
        routes_e, gate_w, up_w, down_w = inputs
        token_e = routes_e // TOP
        slot_rows = tokens_ext[token_e]
        gate_pre = jnp.dot(slot_rows, gate_w, preferred_element_type=jnp.float32)
        up_pre = jnp.dot(slot_rows, up_w, preferred_element_type=jnp.float32)
        hidden = (jax.nn.silu(gate_pre) * up_pre).astype(jnp.bfloat16)
        expert_out = jnp.dot(hidden, down_w, preferred_element_type=jnp.float32).astype(jnp.bfloat16)
        weight_e = gates_ext[routes_e].astype(jnp.float32)
        out_f = expert_out.astype(jnp.float32)
        out_acc = out_acc.at[token_e].add(weight_e[:, None] * out_f)
        grad_rows = grad_ext[token_e].astype(jnp.float32)
        dgate_acc = dgate_acc.at[routes_e].add(jnp.sum(out_f * grad_rows, axis=1))
        scaled = (weight_e[:, None] * grad_rows).astype(jnp.bfloat16)
        d_hidden = jnp.dot(scaled, down_w.T, preferred_element_type=jnp.float32)
        sigma_gate = jax.nn.sigmoid(gate_pre)
        d_up = (d_hidden * gate_pre * sigma_gate).astype(jnp.bfloat16)
        d_gate = (d_hidden * up_pre * sigma_gate * (1.0 + gate_pre * (1.0 - sigma_gate))).astype(jnp.bfloat16)
        d_rows = (jnp.dot(d_gate, gate_w.T, preferred_element_type=jnp.float32)
                  + jnp.dot(d_up, up_w.T, preferred_element_type=jnp.float32)).astype(jnp.bfloat16)
        dx_acc = dx_acc.at[token_e].add(d_rows.astype(jnp.float32))
        group_rows = slot_rows.astype(jnp.float32).reshape(N_DP, N_EXPERT * CAP, D)
        group_scaled = scaled.astype(jnp.float32).reshape(N_DP, N_EXPERT * CAP, D)
        group_gate = d_gate.astype(jnp.float32).reshape(N_DP, N_EXPERT * CAP, FF)
        group_up = d_up.astype(jnp.float32).reshape(N_DP, N_EXPERT * CAP, FF)
        group_hidden = hidden.astype(jnp.float32).reshape(N_DP, N_EXPERT * CAP, FF)
        grad_gate = summed_groups(jnp.einsum("gsd,gsf->gdf", group_rows, group_gate))
        grad_up = summed_groups(jnp.einsum("gsd,gsf->gdf", group_rows, group_up))
        grad_down = summed_groups(jnp.einsum("gsf,gsd->gfd", group_hidden, group_scaled))
        return (out_acc, dx_acc, dgate_acc), (grad_gate, grad_up, grad_down)

    start = (jnp.zeros((TOKENS + 1, D), jnp.float32), jnp.zeros((TOKENS + 1, D), jnp.float32),
             jnp.zeros((route_total + 1,), jnp.float32))
    totals, grads = lax.scan(per_expert, start, (route_of, w_gate, w_up, w_down))
    out_acc, dx_acc, dgate_acc = totals
    mixed_out = out_acc[:TOKENS].astype(jnp.bfloat16)
    d_tokens = dx_acc[:TOKENS].astype(jnp.bfloat16)
    d_gates = dgate_acc[:route_total].reshape(TOKENS, TOP)
    return (mixed_out, d_tokens, d_gates, grads[0], grads[1], grads[2])
```

```python
import functools

import jax
import jax.numpy as jnp
from jax import lax
from jax.experimental import pallas as pl
from jax.experimental.pallas import tpu as pltpu
from jax.sharding import PartitionSpec as P

BF16 = jnp.bfloat16
F32 = jnp.float32
MESH = pl.DeviceIdType.MESH
NN = (((1,), (0,)), ((), ()))
NT = (((1,), (1,)), ((), ()))
TN = (((0,), (0,)), ((), ()))


def dot(spec, a, b):
    return jnp.einsum(spec, a, b, preferred_element_type=F32)


def mm(a, b, dims):
    return lax.dot_general(a, b, dims, preferred_element_type=F32)


def local_wide(tokens, expert_ids, gate_weights, grad_out, w_gate, w_up, w_down):
    tok_dev, model_dim = tokens.shape
    exp_dev = w_gate.shape[0]
    owners = lax.axis_size("expert")
    experts = exp_dev * owners
    chosen = expert_ids[:, :, None] == jnp.arange(experts, dtype=jnp.int32)
    gate_of = jnp.sum(jnp.where(chosen, gate_weights[:, :, None], 0.0), axis=1)
    gates = lax.all_to_all(
        gate_of.reshape(tok_dev, owners, exp_dev).transpose(1, 2, 0), "expert", 0, 0, tiled=True
    )
    gates = gates.transpose(1, 0, 2).reshape(exp_dev, owners * tok_dev, 1)
    rows = lax.all_gather(tokens, "expert", axis=0, tiled=True)
    grads = lax.all_gather(grad_out, "expert", axis=0, tiled=True)
    gate_pre = dot("td,edf->etf", rows, w_gate)
    up_pre = dot("td,edf->etf", rows, w_up)
    d_mid = dot("td,efd->etf", grads, w_down)
    sigma = jax.nn.sigmoid(gate_pre)
    hidden = gate_pre * sigma * up_pre
    d_gate_sum = jnp.sum(hidden * d_mid, axis=2)
    d_hidden = gates * d_mid
    scaled_hidden = (gates * hidden).astype(BF16)
    d_up = (d_hidden * gate_pre * sigma).astype(BF16)
    d_gate = (d_hidden * up_pre * sigma * (1.0 + gate_pre * (1.0 - sigma))).astype(BF16)
    mixed = dot("etf,efd->td", scaled_hidden, w_down).astype(BF16)
    mixed_out = lax.psum_scatter(mixed, "expert", scatter_dimension=0, tiled=True)
    d_rows = (dot("etf,edf->td", d_gate, w_gate) + dot("etf,edf->td", d_up, w_up)).astype(BF16)
    d_tokens = lax.psum_scatter(d_rows, "expert", scatter_dimension=0, tiled=True)
    back = lax.all_to_all(
        d_gate_sum.reshape(exp_dev, owners, tok_dev).transpose(1, 0, 2), "expert", 0, 0, tiled=True
    )
    back = back.reshape(experts, tok_dev).T
    d_gates = jnp.sum(jnp.where(chosen, back[:, None, :], 0.0), axis=2)
    part_gate = dot("td,etf->edf", rows, d_gate).astype(BF16)
    part_up = dot("td,etf->edf", rows, d_up).astype(BF16)
    part_down = dot("etf,td->efd", scaled_hidden, grads).astype(BF16)
    grad_gate = lax.psum_scatter(part_gate, "dp", scatter_dimension=1, tiled=True)
    grad_up = lax.psum_scatter(part_up, "dp", scatter_dimension=1, tiled=True)
    grad_down = lax.psum_scatter(part_down, "dp", scatter_dimension=2, tiled=True)
    return (mixed_out, d_tokens, d_gates, grad_gate, grad_up, grad_down)


def slot_of(step):
    if step == 0:
        return 0
    if abs(step) == 4:
        return 1
    return 2 * step if step > 0 else 1 - 2 * step


def step_of(slot):
    if slot == 0:
        return 0
    if slot == 1:
        return 4
    return slot // 2 if slot % 2 == 0 else -(slot // 2)


RETURN_LEFT = (("m", 4), ("r", 3), ("m", 3), ("r", 2), ("m", 2), ("r", 1), ("m", 1))
RETURN_RIGHT = (("r", 4), ("m", -3), ("r", -3), ("m", -2), ("r", -2), ("m", -1), ("r", -1))


def layer_kernel(
    tok_in, grad_in, wg_in, wu_in, wd_in, ids_ref, gw_ref,
    mixed_ref, dtok_ref, dgates_ref, ogate_ref, oup_ref, odown_ref,
    x_all, g_all, wg, wu, wd, parts_m, parts_r, dgu, mid, dwgu, dwd, landed,
    pr_gu, pr_d, xr_gu, xr_d, gsend, grecv, wcol, dcol, dsend, back,
    local_sem, ag_send, ag_recv, rs_send, rs_recv, small_send, small_recv, dp_send, dp_recv,
):
    n = 8
    tok, model = tok_in.shape
    exp_dev, ff = wg.shape[0], wg.shape[2]
    half = tok // 2
    quarter = model // 4
    me = lax.axis_index("expert")
    dp = lax.axis_index("dp")
    odd = me % 2
    pos = (me // 2) * (1 - odd) + (n - 1 - me // 2) * odd

    def device_at(q):
        q = (q + 2 * n) % n
        far = q // (n // 2)
        return far * (2 * n - 1 - 2 * q) + (1 - far) * 2 * q

    right, left = device_at(pos + 1), device_at(pos - 1)
    core = dp % 2
    xpos = dp // 2
    partner = xpos * 2 + 1 - core
    across = (1 - xpos) * 2 + core
    sides = (right, left)

    barrier = pltpu.get_barrier_semaphore()
    for k in range(1, n):
        pl.semaphore_signal(
            barrier, inc=1, device_id={"expert": device_at(pos + k)}, device_id_type=MESH
        )
    for other in (partner, across):
        pl.semaphore_signal(barrier, inc=1, device_id={"dp": other}, device_id_type=MESH)

    locals_ = [
        pltpu.make_async_copy(tok_in, x_all.at[pl.ds(0, tok)], local_sem.at[0]),
        pltpu.make_async_copy(grad_in, g_all.at[pl.ds(0, tok)], local_sem.at[1]),
        pltpu.make_async_copy(wg_in, wg, local_sem.at[2]),
        pltpu.make_async_copy(wu_in, wu, local_sem.at[3]),
        pltpu.make_async_copy(wd_in, wd, local_sem.at[4]),
    ]
    for copy in locals_:
        copy.start()
    pl.semaphore_wait(barrier, n + 1)

    def send_to(src, dst, side, index):
        return pltpu.make_async_remote_copy(
            src_ref=src, dst_ref=dst,
            send_sem=ag_send.at[side, index], recv_sem=ag_recv.at[side, index],
            device_id={"expert": sides[side]}, device_id_type=MESH,
        )

    def early(side, index):
        hop, part = index // 2, index % 2
        sign = 1 if side == 0 else -1
        buf, own = ((x_all, tok_in), (g_all, grad_in))[side]
        dst = buf.at[pl.ds(slot_of(sign * (hop + 1)) * tok + part * half, half)]
        if hop == 0:
            src = own.at[pl.ds(part * half, half)]
        else:
            src = buf.at[pl.ds(slot_of(sign * hop) * tok + part * half, half)]
        return send_to(src, dst, side, index)

    def late(side, hop, part):
        if side == 0:
            buf, s, d = g_all, 2 * hop, 2 * hop + 2
        else:
            buf, s, d = x_all, 2 * hop + (hop + 2) // 3, 2 * hop + 3
        return send_to(
            buf.at[pl.ds(s * tok + part * half, half)],
            buf.at[pl.ds(d * tok + part * half, half)],
            side, 8 + 2 * hop + part,
        )

    for part in range(2):
        for side in range(2):
            early(side, part).start()

    lane = lax.broadcasted_iota(jnp.int32, (tok, 128), 1)
    expert_of_lane = jnp.where(lane % 8 < exp_dev, (lane // 8) * exp_dev + lane % 8, -1)
    gates = jnp.zeros((tok, 128), F32)
    for k in range(ids_ref.shape[1]):
        gates = gates + jnp.where(ids_ref[:, k : k + 1] == expert_of_lane, gw_ref[:, k : k + 1], 0.0)
    gsend[...] = jnp.transpose(gates)[: n * 8].reshape(n, 8, 128)

    def gate_copy(k):
        slot = slot_of(k if k <= 4 else k - 8)
        to = device_at(pos + k)
        return pltpu.make_async_remote_copy(
            src_ref=gsend.at[to], dst_ref=grecv.at[slot],
            send_sem=small_send.at[0, slot], recv_sem=small_recv.at[0, slot],
            device_id={"expert": to}, device_id_type=MESH,
        )

    for k in range(1, n):
        gate_copy(k).start()
    grecv[0] = gsend[me]
    locals_[0].wait()
    locals_[1].wait()

    for index in range(8):
        for side in range(2):
            early(side, index).wait_recv()
            if index < 6:
                early(side, index + 2).start()
            else:
                late(side, 0, index - 6).start()
        if index == 1:
            for k in range(1, n):
                gate_copy(k).wait_recv()
            cols = jnp.concatenate(
                [grecv[...].reshape(n * 8, 128), jnp.zeros((128 - n * 8, 128), F32)], axis=0
            )
            cols = jnp.transpose(cols)
            for slot in range(n):
                for e in range(exp_dev):
                    at = slot * 8 + e
                    wcol[e, pl.ds(slot * tok, tok), :] = jnp.broadcast_to(
                        cols[:, at : at + 1], (tok, 128)
                    )
        if index == 3:
            for copy in locals_[2:]:
                copy.wait()

    bufs = {"m": parts_m, "r": parts_r}
    orders = (RETURN_RIGHT, RETURN_LEFT)

    def back_copy(side, index):
        kind, step = orders[side][index]
        return pltpu.make_async_remote_copy(
            src_ref=bufs[kind].at[pl.ds(slot_of(step) * tok, tok)], dst_ref=landed.at[side, index],
            send_sem=rs_send.at[side, index], recv_sem=rs_recv.at[side, index],
            device_id={"expert": sides[side]}, device_id_type=MESH,
        )

    def stage_one(j):
        rows = pl.ds(pl.multiple_of(j * 2 * tok, 2 * tok), 2 * tok)
        for e in range(exp_dev):
            gate_pre = mm(x_all[rows, :], wg[e], NN)
            up_pre = mm(x_all[rows, :], wu[e], NN)
            d_mid = mm(g_all[rows, :], wd[pl.ds(e * ff, ff), :], NT)
            weight = wcol[e, rows, 0:1]
            sigma = jax.nn.sigmoid(gate_pre)
            hidden = gate_pre * sigma * up_pre
            dots = jnp.sum(hidden * d_mid, axis=1, keepdims=True)
            dcol[e, rows, :] = jnp.broadcast_to(dots, (2 * tok, 128))
            d_hidden = weight * d_mid
            mid[rows, pl.ds(e * ff, ff)] = (weight * hidden).astype(BF16)
            dgu[rows, pl.ds((exp_dev + e) * ff, ff)] = (d_hidden * gate_pre * sigma).astype(BF16)
            dgu[rows, pl.ds(e * ff, ff)] = (
                d_hidden * up_pre * sigma * (1.0 + gate_pre * (1.0 - sigma))
            ).astype(BF16)

    def stage_two(j):
        rows = pl.ds(pl.multiple_of(j * 2 * tok, 2 * tok), 2 * tok)

        def tile(t, carry):
            cols = pl.ds(pl.multiple_of(t * 512, 512), 512)
            parts_m[rows, cols] = mm(mid[rows, :], wd[:, cols], NN).astype(BF16)
            total = None
            for e in range(exp_dev):
                for w, base in ((wg, 0), (wu, exp_dev)):
                    term = mm(dgu[rows, pl.ds((base + e) * ff, ff)], w[e, cols, :], NT)
                    total = term if total is None else total + term
            parts_r[rows, cols] = total.astype(BF16)
            return carry

        lax.fori_loop(0, model // 512, tile, 0)

    def pair(j, carry):
        stage_one(j)
        for part in range(2):
            @pl.when(j < 3)
            def _():
                for side in range(2):
                    late(side, j, part).wait_recv()

            @pl.when(j < 2)
            def _():
                for side in range(2):
                    late(side, j + 1, part).start()

            if part == 0:
                stage_two(j)

        @pl.when(j == 1)
        def _():
            for side in range(2):
                back_copy(side, 0).start()

        return carry

    lax.fori_loop(0, 4, pair, 0)
    for side in range(2):
        back_copy(side, 1).start()

    stacked = jnp.zeros((tok, 128), F32)
    for slot in range(n):
        for e in range(exp_dev):
            stacked = jnp.where(lane == slot * 8 + e, dcol[e, pl.ds(slot * tok, tok), :], stacked)
    dsend[...] = jnp.transpose(stacked)[: n * 8].reshape(n, 8, 128)

    def dots_copy(slot):
        return pltpu.make_async_remote_copy(
            src_ref=dsend.at[slot], dst_ref=back.at[me],
            send_sem=small_send.at[1, slot], recv_sem=small_recv.at[1, slot],
            device_id={"expert": device_at(pos - step_of(slot))}, device_id_type=MESH,
        )

    for slot in range(1, n):
        dots_copy(slot).start()
    own_dots = pltpu.make_async_copy(dsend.at[0], back.at[me], local_sem.at[0])
    own_dots.start()

    def piece_rows(piece):
        return pl.ds(pl.multiple_of(piece * quarter, quarter), quarter)

    def weight_grads(piece):
        def tile(t, carry):
            base = pl.multiple_of(piece * quarter + t * 256, 256)
            for c in range(2):
                cols = pl.ds(c * exp_dev * ff, exp_dev * ff)
                dwgu[pl.ds(base, 256), cols] = mm(
                    x_all[:, pl.ds(base, 256)], dgu[:, cols], TN
                ).astype(BF16)
            return carry

        lax.fori_loop(0, quarter // 256, tile, 0)

        def tile_down(t, carry):
            at = pl.multiple_of(t * 256, 256)
            dwd[piece, pl.ds(at, 256), :] = mm(
                mid[:, pl.ds(at, 256)], g_all[:, piece_rows(piece)], TN
            ).astype(BF16)
            return carry

        lax.fori_loop(0, exp_dev * ff // 256, tile_down, 0)

    def swap_copies(piece, where):
        return [
            pltpu.make_async_remote_copy(
                src_ref=src, dst_ref=dst, send_sem=dp_send.at[at], recv_sem=dp_recv.at[at],
                device_id={"dp": partner}, device_id_type=MESH,
            )
            for src, dst, at in (
                (dwgu.at[piece_rows(piece)], pr_gu.at[where], 2 * where),
                (dwd.at[piece], pr_d.at[where], 2 * where + 1),
            )
        ]

    far_own, far_partner = (1 - xpos) * 2 + core, (1 - xpos) * 2 + 1 - core
    near_own, near_partner = xpos * 2 + core, xpos * 2 + 1 - core
    far_swap = swap_copies(far_partner, 0)
    near_swap = swap_copies(near_partner, 1)
    far_send = [
        pltpu.make_async_remote_copy(
            src_ref=src, dst_ref=dst, send_sem=dp_send.at[at], recv_sem=dp_recv.at[at],
            device_id={"dp": across}, device_id_type=MESH,
        )
        for src, dst, at in (
            (dwgu.at[piece_rows(far_own)], xr_gu, 4),
            (dwd.at[far_own], xr_d, 5),
        )
    ]

    def return_step(index):
        for side in range(2):
            kind, step = orders[side][index]
            buf, base = bufs[kind], slot_of(step) * tok
            back_copy(side, index - 2).wait_recv()

            def add(t, carry):
                rows = pl.ds(pl.multiple_of(base + t * 32, 32), 32)
                got = landed[side, index - 2, pl.ds(pl.multiple_of(t * 32, 32), 32), :]
                buf[rows, :] = (buf[rows, :].astype(F32) + got.astype(F32)).astype(BF16)
                return carry

            lax.fori_loop(0, tok // 32, add, 0)
            back_copy(side, index).start()

    weight_grads(far_partner)
    for copy in far_swap:
        copy.start()
    return_step(2)
    weight_grads(far_own)
    for copy in far_swap:
        copy.wait_recv()

    def add_far(t, carry):
        rows = pl.ds(pl.multiple_of(far_own * quarter + t * 32, 32), 32)
        got = pr_gu[0, pl.ds(pl.multiple_of(t * 32, 32), 32), :]
        dwgu[rows, :] = (dwgu[rows, :].astype(F32) + got.astype(F32)).astype(BF16)
        return carry

    lax.fori_loop(0, quarter // 32, add_far, 0)
    far_send[0].start()

    def add_far_down(t, carry):
        rows = pl.ds(pl.multiple_of(t * 32, 32), 32)
        dwd[far_own, rows, :] = (
            dwd[far_own, rows, :].astype(F32) + pr_d[0, rows, :].astype(F32)
        ).astype(BF16)
        return carry

    lax.fori_loop(0, exp_dev * ff // 32, add_far_down, 0)
    far_send[1].start()
    return_step(3)
    weight_grads(near_partner)
    for copy in near_swap:
        copy.start()
    return_step(4)
    weight_grads(near_own)
    return_step(5)

    own_dots.wait()
    for slot in range(1, n):
        dots_copy(slot).wait_recv()
    got = jnp.concatenate(
        [back[...].reshape(n * 8, 128), jnp.zeros((128 - n * 8, 128), F32)], axis=0
    )
    got = jnp.transpose(got)
    result = jnp.zeros((tok, 128), F32)
    for k in range(ids_ref.shape[1]):
        mine = jnp.sum(
            jnp.where(ids_ref[:, k : k + 1] == expert_of_lane, got, 0.0), axis=1, keepdims=True
        )
        result = jnp.where(lane == k, mine, result)
    dgates_ref[...] = result[:, : ids_ref.shape[1]]
    return_step(6)

    for copy in near_swap:
        copy.wait_recv()
    for copy in far_send:
        copy.wait_recv()

    def final_gu(t, carry):
        rows = pl.ds(pl.multiple_of(t * 32, 32), 32)
        own = pl.ds(pl.multiple_of(near_own * quarter + t * 32, 32), 32)
        total = (
            dwgu[own, :].astype(F32) + pr_gu[1, rows, :].astype(F32) + xr_gu[rows, :].astype(F32)
        ).astype(BF16)
        for e in range(exp_dev):
            ogate_ref[e, rows, :] = total[:, e * ff : (e + 1) * ff]
            oup_ref[e, rows, :] = total[:, (exp_dev + e) * ff : (exp_dev + e + 1) * ff]
        return carry

    lax.fori_loop(0, quarter // 32, final_gu, 0)
    for e in range(exp_dev):
        def final_down(t, carry):
            at = pl.multiple_of(t * 32, 32)
            rows = pl.ds(pl.multiple_of(e * ff + at, 32), 32)
            odown_ref[e, pl.ds(at, 32), :] = (
                dwd[near_own, rows, :].astype(F32)
                + pr_d[1, rows, :].astype(F32)
                + xr_d[rows, :].astype(F32)
            ).astype(BF16)
            return carry

        lax.fori_loop(0, ff // 32, final_down, 0)

    for index in (5, 6):
        for side in range(2):
            back_copy(side, index).wait_recv()
        kind = orders[0][index][0]
        other = orders[1][index][0]
        for side, name in ((0, kind), (1, other)):
            buf, out = bufs[name], {"m": mixed_ref, "r": dtok_ref}[name]

            def close(t, carry):
                rows = pl.ds(pl.multiple_of(t * 32, 32), 32)
                so_far = buf if index == 5 else out
                out[rows, :] = (
                    so_far[rows, :].astype(F32) + landed[side, index, rows, :].astype(F32)
                ).astype(BF16)
                return carry

            lax.fori_loop(0, tok // 32, close, 0)

    for side in range(2):
        for index in range(8):
            early(side, index).wait_send()
        for hop in range(3):
            for part in range(2):
                late(side, hop, part).wait_send()
        for index in range(7):
            back_copy(side, index).wait_send()
    for k in range(1, n):
        gate_copy(k).wait_send()
        dots_copy(k).wait_send()
    for copy in far_swap + near_swap + far_send:
        copy.wait_send()


def local(tokens, expert_ids, gate_weights, grad_out, w_gate, w_up, w_down):
    owners, dps = lax.axis_size("expert"), lax.axis_size("dp")
    if owners != 8 or dps != 4:
        return local_wide(tokens, expert_ids, gate_weights, grad_out, w_gate, w_up, w_down)
    tok, model = tokens.shape
    exp_dev, _, ff = w_gate.shape
    rows, mids = owners * tok, exp_dev * ff
    quarter = model // dps
    hbm = pl.BlockSpec(memory_space=pl.ANY)
    vmem = pl.BlockSpec(memory_space=pltpu.VMEM)
    dma = pltpu.SemaphoreType.DMA
    out = pl.pallas_call(
        layer_kernel,
        out_shape=(
            jax.ShapeDtypeStruct((tok, model), BF16),
            jax.ShapeDtypeStruct((tok, model), BF16),
            jax.ShapeDtypeStruct(gate_weights.shape, F32),
            jax.ShapeDtypeStruct((exp_dev, quarter, ff), BF16),
            jax.ShapeDtypeStruct((exp_dev, quarter, ff), BF16),
            jax.ShapeDtypeStruct((exp_dev, ff, quarter), BF16),
        ),
        in_specs=[hbm] * 5 + [vmem] * 2,
        out_specs=[vmem] * 6,
        scratch_shapes=[
            pltpu.VMEM((rows, model), BF16),
            pltpu.VMEM((rows, model), BF16),
            pltpu.VMEM((exp_dev, model, ff), BF16),
            pltpu.VMEM((exp_dev, model, ff), BF16),
            pltpu.VMEM((mids, model), BF16),
            pltpu.VMEM((rows, model), BF16),
            pltpu.VMEM((rows, model), BF16),
            pltpu.VMEM((rows, 2 * mids), BF16),
            pltpu.VMEM((rows, mids), BF16),
            pltpu.VMEM((model, 2 * mids), BF16),
            pltpu.VMEM((dps, mids, quarter), BF16),
            pltpu.VMEM((2, 7, tok, model), BF16),
            pltpu.VMEM((2, quarter, 2 * mids), BF16),
            pltpu.VMEM((2, mids, quarter), BF16),
            pltpu.VMEM((quarter, 2 * mids), BF16),
            pltpu.VMEM((mids, quarter), BF16),
            pltpu.VMEM((owners, 8, 128), F32),
            pltpu.VMEM((owners, 8, 128), F32),
            pltpu.VMEM((exp_dev, rows, 128), F32),
            pltpu.VMEM((exp_dev, rows, 128), F32),
            pltpu.VMEM((owners, 8, 128), F32),
            pltpu.VMEM((owners, 8, 128), F32),
            dma((5,)),
            dma((2, 14)),
            dma((2, 14)),
            dma((2, 7)),
            dma((2, 7)),
            dma((2, 8)),
            dma((2, 8)),
            dma((6,)),
            dma((6,)),
        ],
        compiler_params=pltpu.CompilerParams(
            collective_id=0, has_side_effects=True, vmem_limit_bytes=67_043_328
        ),
        name="moe_layer",
    )(tokens, grad_out, w_gate, w_up, w_down.reshape(mids, model), expert_ids, gate_weights)
    return tuple(out)


def solution(mesh):
    in_specs = (
        P(("dp", "expert"), None),
        P(("dp", "expert"), None),
        P(("dp", "expert"), None),
        P(("dp", "expert"), None),
        P("expert", None, None),
        P("expert", None, None),
        P("expert", None, None),
    )
    out_specs = (
        P(("dp", "expert"), None),
        P(("dp", "expert"), None),
        P(("dp", "expert"), None),
        P("expert", "dp", None),
        P("expert", "dp", None),
        P("expert", None, "dp"),
    )
    return jax.shard_map(local, mesh=mesh, in_specs=in_specs, out_specs=out_specs, check_vma=False)
```

```python
import functools

import jax
import jax.numpy as jnp
from jax import lax
from jax.experimental import pallas as pl
from jax.experimental.pallas import tpu as pltpu
from jax.sharding import PartitionSpec as P

BF16 = jnp.bfloat16
F32 = jnp.float32
MESH = pl.DeviceIdType.MESH
NN = (((1,), (0,)), ((), ()))
NT = (((1,), (1,)), ((), ()))
TN = (((0,), (0,)), ((), ()))


def dot(spec, a, b):
    return jnp.einsum(spec, a, b, preferred_element_type=F32)


def mm(a, b, dims):
    return lax.dot_general(a, b, dims, preferred_element_type=F32)


def local_wide(tokens, expert_ids, gate_weights, grad_out, w_gate, w_up, w_down):
    tok_dev, model_dim = tokens.shape
    exp_dev = w_gate.shape[0]
    owners = lax.axis_size("expert")
    experts = exp_dev * owners
    chosen = expert_ids[:, :, None] == jnp.arange(experts, dtype=jnp.int32)
    gate_of = jnp.sum(jnp.where(chosen, gate_weights[:, :, None], 0.0), axis=1)
    gates = lax.all_to_all(
        gate_of.reshape(tok_dev, owners, exp_dev).transpose(1, 2, 0), "expert", 0, 0, tiled=True
    )
    gates = gates.transpose(1, 0, 2).reshape(exp_dev, owners * tok_dev, 1)
    rows = lax.all_gather(tokens, "expert", axis=0, tiled=True)
    grads = lax.all_gather(grad_out, "expert", axis=0, tiled=True)
    gate_pre = dot("td,edf->etf", rows, w_gate)
    up_pre = dot("td,edf->etf", rows, w_up)
    d_mid = dot("td,efd->etf", grads, w_down)
    sigma = jax.nn.sigmoid(gate_pre)
    hidden = gate_pre * sigma * up_pre
    d_gate_sum = jnp.sum(hidden * d_mid, axis=2)
    d_hidden = gates * d_mid
    scaled_hidden = (gates * hidden).astype(BF16)
    d_up = (d_hidden * gate_pre * sigma).astype(BF16)
    d_gate = (d_hidden * up_pre * sigma * (1.0 + gate_pre * (1.0 - sigma))).astype(BF16)
    mixed = dot("etf,efd->td", scaled_hidden, w_down).astype(BF16)
    mixed_out = lax.psum_scatter(mixed, "expert", scatter_dimension=0, tiled=True)
    d_rows = (dot("etf,edf->td", d_gate, w_gate) + dot("etf,edf->td", d_up, w_up)).astype(BF16)
    d_tokens = lax.psum_scatter(d_rows, "expert", scatter_dimension=0, tiled=True)
    back = lax.all_to_all(
        d_gate_sum.reshape(exp_dev, owners, tok_dev).transpose(1, 0, 2), "expert", 0, 0, tiled=True
    )
    back = back.reshape(experts, tok_dev).T
    d_gates = jnp.sum(jnp.where(chosen, back[:, None, :], 0.0), axis=2)
    part_gate = dot("td,etf->edf", rows, d_gate).astype(BF16)
    part_up = dot("td,etf->edf", rows, d_up).astype(BF16)
    part_down = dot("etf,td->efd", scaled_hidden, grads).astype(BF16)
    grad_gate = lax.psum_scatter(part_gate, "dp", scatter_dimension=1, tiled=True)
    grad_up = lax.psum_scatter(part_up, "dp", scatter_dimension=1, tiled=True)
    grad_down = lax.psum_scatter(part_down, "dp", scatter_dimension=2, tiled=True)
    return (mixed_out, d_tokens, d_gates, grad_gate, grad_up, grad_down)


def slot_of(step):
    if step == 0:
        return 0
    if abs(step) == 4:
        return 1
    return 2 * step if step > 0 else 1 - 2 * step


def step_of(slot):
    if slot == 0:
        return 0
    if slot == 1:
        return 4
    return slot // 2 if slot % 2 == 0 else -(slot // 2)


RETURN_LEFT = (("m", 4), ("r", 3), ("m", 3), ("r", 2), ("m", 2), ("r", 1), ("m", 1))
RETURN_RIGHT = (("r", 4), ("m", -3), ("r", -3), ("m", -2), ("r", -2), ("m", -1), ("r", -1))


def layer_kernel(
    tok_in, grad_in, wg_in, wu_in, wd_in, ids_ref, gw_ref,
    mixed_ref, dtok_ref, dgates_ref, ogate_ref, oup_ref, odown_ref,
    x_all, g_all, wg, wu, wd, parts_m, parts_r, dgu, mid, dwgu, dwd, landed,
    pr_gu, pr_d, xr_gu, xr_d, gsend, grecv, wcol, dcol, dsend, back,
    local_sem, ag_send, ag_recv, rs_send, rs_recv, small_send, small_recv, dp_send, dp_recv,
):
    n = 8
    tok, model = tok_in.shape
    exp_dev, ff = wg.shape[0], wg.shape[2]
    half = tok // 2
    quarter = model // 4
    me = lax.axis_index("expert")
    dp = lax.axis_index("dp")
    odd = me % 2
    pos = (me // 2) * (1 - odd) + (n - 1 - me // 2) * odd

    def device_at(q):
        q = (q + 2 * n) % n
        far = q // (n // 2)
        return far * (2 * n - 1 - 2 * q) + (1 - far) * 2 * q

    right, left = device_at(pos + 1), device_at(pos - 1)
    core = dp % 2
    xpos = dp // 2
    partner = xpos * 2 + 1 - core
    across = (1 - xpos) * 2 + core
    sides = (right, left)

    barrier = pltpu.get_barrier_semaphore()
    for k in range(1, n):
        pl.semaphore_signal(
            barrier, inc=1, device_id={"expert": device_at(pos + k)}, device_id_type=MESH
        )
    for other in (partner, across):
        pl.semaphore_signal(barrier, inc=1, device_id={"dp": other}, device_id_type=MESH)

    locals_ = [
        pltpu.make_async_copy(tok_in, x_all.at[pl.ds(0, tok)], local_sem.at[0]),
        pltpu.make_async_copy(grad_in, g_all.at[pl.ds(0, tok)], local_sem.at[1]),
        pltpu.make_async_copy(wg_in, wg, local_sem.at[2]),
        pltpu.make_async_copy(wu_in, wu, local_sem.at[3]),
        pltpu.make_async_copy(wd_in, wd, local_sem.at[4]),
    ]
    for copy in locals_:
        copy.start()
    pl.semaphore_wait(barrier, n + 1)

    def send_to(src, dst, side, index):
        return pltpu.make_async_remote_copy(
            src_ref=src, dst_ref=dst,
            send_sem=ag_send.at[side, index], recv_sem=ag_recv.at[side, index],
            device_id={"expert": sides[side]}, device_id_type=MESH,
        )

    def early(side, index):
        hop, part = index // 2, index % 2
        sign = 1 if side == 0 else -1
        buf, own = ((x_all, tok_in), (g_all, grad_in))[side]
        dst = buf.at[pl.ds(slot_of(sign * (hop + 1)) * tok + part * half, half)]
        if hop == 0:
            src = own.at[pl.ds(part * half, half)]
        else:
            src = buf.at[pl.ds(slot_of(sign * hop) * tok + part * half, half)]
        return send_to(src, dst, side, index)

    def late(side, hop, part):
        if side == 0:
            buf, s, d = g_all, 2 * hop, 2 * hop + 2
        else:
            buf, s, d = x_all, 2 * hop + (hop + 2) // 3, 2 * hop + 3
        return send_to(
            buf.at[pl.ds(s * tok + part * half, half)],
            buf.at[pl.ds(d * tok + part * half, half)],
            side, 8 + 2 * hop + part,
        )

    for part in range(2):
        for side in range(2):
            early(side, part).start()

    line = lax.broadcasted_iota(jnp.int32, (n * 8, tok), 0)
    expert_of_line = jnp.where(line % 8 < exp_dev, (line // 8) * exp_dev + line % 8, -1)
    top = ids_ref.shape[0]
    gates = jnp.zeros((n * 8, tok), F32)
    for k in range(top):
        gates = gates + jnp.where(ids_ref[k : k + 1, :] == expert_of_line, gw_ref[k : k + 1, :], 0.0)
    gsend[...] = gates.reshape(n, 8, tok)

    def gate_copy(k):
        slot = slot_of(k if k <= 4 else k - 8)
        to = device_at(pos + k)
        return pltpu.make_async_remote_copy(
            src_ref=gsend.at[to], dst_ref=grecv.at[slot],
            send_sem=small_send.at[0, slot], recv_sem=small_recv.at[0, slot],
            device_id={"expert": to}, device_id_type=MESH,
        )

    for k in range(1, n):
        gate_copy(k).start()
    grecv[0] = gsend[me]
    locals_[0].wait()
    locals_[1].wait()

    for index in range(8):
        for side in range(2):
            early(side, index).wait_recv()
            if index < 6:
                early(side, index + 2).start()
            else:
                late(side, 0, index - 6).start()
        if index == 1:
            for k in range(1, n):
                gate_copy(k).wait_recv()
            cols = jnp.concatenate(
                [grecv[...].reshape(n * 8, 128), jnp.zeros((128 - n * 8, 128), F32)], axis=0
            )
            cols = jnp.transpose(cols)
            for slot in range(n):
                for e in range(exp_dev):
                    at = slot * 8 + e
                    wcol[e, pl.ds(slot * tok, tok), :] = jnp.broadcast_to(
                        cols[:, at : at + 1], (tok, 128)
                    )
        if index == 3:
            for copy in locals_[2:]:
                copy.wait()

    bufs = {"m": parts_m, "r": parts_r}
    orders = (RETURN_RIGHT, RETURN_LEFT)

    def back_copy(side, index):
        kind, step = orders[side][index]
        return pltpu.make_async_remote_copy(
            src_ref=bufs[kind].at[pl.ds(slot_of(step) * tok, tok)], dst_ref=landed.at[side, index],
            send_sem=rs_send.at[side, index], recv_sem=rs_recv.at[side, index],
            device_id={"expert": sides[side]}, device_id_type=MESH,
        )

    def stage_one(j):
        rows = pl.ds(pl.multiple_of(j * 2 * tok, 2 * tok), 2 * tok)
        for e in range(exp_dev):
            gate_pre = mm(x_all[rows, :], wg[e], NN)
            up_pre = mm(x_all[rows, :], wu[e], NN)
            d_mid = mm(g_all[rows, :], wd[pl.ds(e * ff, ff), :], NT)
            weight = wcol[e, rows, 0:1]
            sigma = jax.nn.sigmoid(gate_pre)
            hidden = gate_pre * sigma * up_pre
            dots = jnp.sum(hidden * d_mid, axis=1, keepdims=True)
            dcol[e, rows, :] = jnp.broadcast_to(dots, (2 * tok, 128))
            d_hidden = weight * d_mid
            mid[rows, pl.ds(e * ff, ff)] = (weight * hidden).astype(BF16)
            dgu[rows, pl.ds((exp_dev + e) * ff, ff)] = (d_hidden * gate_pre * sigma).astype(BF16)
            dgu[rows, pl.ds(e * ff, ff)] = (
                d_hidden * up_pre * sigma * (1.0 + gate_pre * (1.0 - sigma))
            ).astype(BF16)

    def stage_two(j):
        rows = pl.ds(pl.multiple_of(j * 2 * tok, 2 * tok), 2 * tok)

        def tile(t, carry):
            cols = pl.ds(pl.multiple_of(t * 512, 512), 512)
            parts_m[rows, cols] = mm(mid[rows, :], wd[:, cols], NN).astype(BF16)
            total = None
            for e in range(exp_dev):
                for w, base in ((wg, 0), (wu, exp_dev)):
                    term = mm(dgu[rows, pl.ds((base + e) * ff, ff)], w[e, cols, :], NT)
                    total = term if total is None else total + term
            parts_r[rows, cols] = total.astype(BF16)
            return carry

        lax.fori_loop(0, model // 512, tile, 0)

    def pair(j, carry):
        stage_one(j)
        for part in range(2):
            @pl.when(j < 3)
            def _():
                for side in range(2):
                    late(side, j, part).wait_recv()

            @pl.when(j < 2)
            def _():
                for side in range(2):
                    late(side, j + 1, part).start()

            if part == 0:
                stage_two(j)

        @pl.when(j == 1)
        def _():
            for side in range(2):
                back_copy(side, 0).start()

        return carry

    lax.fori_loop(0, 4, pair, 0)
    for side in range(2):
        back_copy(side, 1).start()

    lane = lax.broadcasted_iota(jnp.int32, (tok, 128), 1)
    stacked = jnp.zeros((tok, 128), F32)
    for slot in range(n):
        for e in range(exp_dev):
            stacked = jnp.where(lane == slot * 8 + e, dcol[e, pl.ds(slot * tok, tok), :], stacked)
    dsend[...] = jnp.transpose(stacked)[: n * 8].reshape(n, 8, 128)

    def dots_copy(slot):
        return pltpu.make_async_remote_copy(
            src_ref=dsend.at[slot], dst_ref=back.at[me],
            send_sem=small_send.at[1, slot], recv_sem=small_recv.at[1, slot],
            device_id={"expert": device_at(pos - step_of(slot))}, device_id_type=MESH,
        )

    for slot in range(1, n):
        dots_copy(slot).start()
    own_dots = pltpu.make_async_copy(dsend.at[0], back.at[me], local_sem.at[0])
    own_dots.start()

    def piece_rows(piece):
        return pl.ds(pl.multiple_of(piece * quarter, quarter), quarter)

    def weight_grads(piece):
        def tile(t, carry):
            base = pl.multiple_of(piece * quarter + t * 256, 256)
            for c in range(2):
                cols = pl.ds(c * exp_dev * ff, exp_dev * ff)
                dwgu[pl.ds(base, 256), cols] = mm(
                    x_all[:, pl.ds(base, 256)], dgu[:, cols], TN
                ).astype(BF16)
            return carry

        lax.fori_loop(0, quarter // 256, tile, 0)

        def tile_down(t, carry):
            at = pl.multiple_of(t * 256, 256)
            dwd[piece, pl.ds(at, 256), :] = mm(
                mid[:, pl.ds(at, 256)], g_all[:, piece_rows(piece)], TN
            ).astype(BF16)
            return carry

        lax.fori_loop(0, exp_dev * ff // 256, tile_down, 0)

    def swap_copies(piece, where):
        return [
            pltpu.make_async_remote_copy(
                src_ref=src, dst_ref=dst, send_sem=dp_send.at[at], recv_sem=dp_recv.at[at],
                device_id={"dp": partner}, device_id_type=MESH,
            )
            for src, dst, at in (
                (dwgu.at[piece_rows(piece)], pr_gu.at[where], 2 * where),
                (dwd.at[piece], pr_d.at[where], 2 * where + 1),
            )
        ]

    far_own, far_partner = (1 - xpos) * 2 + core, (1 - xpos) * 2 + 1 - core
    near_own, near_partner = xpos * 2 + core, xpos * 2 + 1 - core
    far_swap = swap_copies(far_partner, 0)
    near_swap = swap_copies(near_partner, 1)
    far_send = [
        pltpu.make_async_remote_copy(
            src_ref=src, dst_ref=dst, send_sem=dp_send.at[at], recv_sem=dp_recv.at[at],
            device_id={"dp": across}, device_id_type=MESH,
        )
        for src, dst, at in (
            (dwgu.at[piece_rows(far_own)], xr_gu, 4),
            (dwd.at[far_own], xr_d, 5),
        )
    ]

    def return_step(index):
        for side in range(2):
            kind, step = orders[side][index]
            buf, base = bufs[kind], slot_of(step) * tok
            back_copy(side, index - 2).wait_recv()

            def add(t, carry):
                rows = pl.ds(pl.multiple_of(base + t * 32, 32), 32)
                got = landed[side, index - 2, pl.ds(pl.multiple_of(t * 32, 32), 32), :]
                buf[rows, :] = (buf[rows, :].astype(F32) + got.astype(F32)).astype(BF16)
                return carry

            lax.fori_loop(0, tok // 32, add, 0)
            back_copy(side, index).start()

    weight_grads(far_partner)
    for copy in far_swap:
        copy.start()
    return_step(2)
    weight_grads(far_own)
    for copy in far_swap:
        copy.wait_recv()

    def add_far(t, carry):
        rows = pl.ds(pl.multiple_of(far_own * quarter + t * 32, 32), 32)
        got = pr_gu[0, pl.ds(pl.multiple_of(t * 32, 32), 32), :]
        dwgu[rows, :] = (dwgu[rows, :].astype(F32) + got.astype(F32)).astype(BF16)
        return carry

    lax.fori_loop(0, quarter // 32, add_far, 0)
    far_send[0].start()

    def add_far_down(t, carry):
        rows = pl.ds(pl.multiple_of(t * 32, 32), 32)
        dwd[far_own, rows, :] = (
            dwd[far_own, rows, :].astype(F32) + pr_d[0, rows, :].astype(F32)
        ).astype(BF16)
        return carry

    lax.fori_loop(0, exp_dev * ff // 32, add_far_down, 0)
    far_send[1].start()
    return_step(3)
    weight_grads(near_partner)
    for copy in near_swap:
        copy.start()
    return_step(4)
    weight_grads(near_own)
    return_step(5)

    own_dots.wait()
    for slot in range(1, n):
        dots_copy(slot).wait_recv()
    got = back[...].reshape(n * 8, tok)
    for k in range(top):
        dgates_ref[k : k + 1, :] = jnp.sum(
            jnp.where(ids_ref[k : k + 1, :] == expert_of_line, got, 0.0), axis=0, keepdims=True
        )
    return_step(6)

    for copy in near_swap:
        copy.wait_recv()
    for copy in far_send:
        copy.wait_recv()

    def final_gu(t, carry):
        rows = pl.ds(pl.multiple_of(t * 32, 32), 32)
        own = pl.ds(pl.multiple_of(near_own * quarter + t * 32, 32), 32)
        total = (
            dwgu[own, :].astype(F32) + pr_gu[1, rows, :].astype(F32) + xr_gu[rows, :].astype(F32)
        ).astype(BF16)
        for e in range(exp_dev):
            ogate_ref[e, rows, :] = total[:, e * ff : (e + 1) * ff]
            oup_ref[e, rows, :] = total[:, (exp_dev + e) * ff : (exp_dev + e + 1) * ff]
        return carry

    lax.fori_loop(0, quarter // 32, final_gu, 0)
    for e in range(exp_dev):
        def final_down(t, carry):
            at = pl.multiple_of(t * 32, 32)
            rows = pl.ds(pl.multiple_of(e * ff + at, 32), 32)
            odown_ref[e, pl.ds(at, 32), :] = (
                dwd[near_own, rows, :].astype(F32)
                + pr_d[1, rows, :].astype(F32)
                + xr_d[rows, :].astype(F32)
            ).astype(BF16)
            return carry

        lax.fori_loop(0, ff // 32, final_down, 0)

    for index in (5, 6):
        for side in range(2):
            back_copy(side, index).wait_recv()
        kind = orders[0][index][0]
        other = orders[1][index][0]
        for side, name in ((0, kind), (1, other)):
            buf, out = bufs[name], {"m": mixed_ref, "r": dtok_ref}[name]

            def close(t, carry):
                rows = pl.ds(pl.multiple_of(t * 32, 32), 32)
                so_far = buf if index == 5 else out
                out[rows, :] = (
                    so_far[rows, :].astype(F32) + landed[side, index, rows, :].astype(F32)
                ).astype(BF16)
                return carry

            lax.fori_loop(0, tok // 32, close, 0)

    for side in range(2):
        for index in range(8):
            early(side, index).wait_send()
        for hop in range(3):
            for part in range(2):
                late(side, hop, part).wait_send()
        for index in range(7):
            back_copy(side, index).wait_send()
    for k in range(1, n):
        gate_copy(k).wait_send()
        dots_copy(k).wait_send()
    for copy in far_swap + near_swap + far_send:
        copy.wait_send()


def hand_over(*refs):
    held, sem = refs[12:18], refs[18]
    inward = [pltpu.make_async_copy(refs[i], held[i], sem.at[0, i]) for i in range(6)]
    outward = [pltpu.make_async_copy(held[i], refs[6 + i], sem.at[1, i]) for i in range(6)]
    for copy in inward:
        copy.start()
    for i in range(6):
        inward[i].wait()
        outward[i].start()
    for copy in outward:
        copy.wait()


def local(tokens, expert_ids, gate_weights, grad_out, w_gate, w_up, w_down):
    owners, dps = lax.axis_size("expert"), lax.axis_size("dp")
    if owners != 8 or dps != 4:
        return local_wide(tokens, expert_ids, gate_weights, grad_out, w_gate, w_up, w_down)
    tok, model = tokens.shape
    exp_dev, _, ff = w_gate.shape
    rows, mids = owners * tok, exp_dev * ff
    quarter = model // dps
    hbm = pl.BlockSpec(memory_space=pl.ANY)
    vmem = pl.BlockSpec(memory_space=pltpu.VMEM)
    dma = pltpu.SemaphoreType.DMA
    out = pl.pallas_call(
        layer_kernel,
        out_shape=(
            jax.ShapeDtypeStruct((tok, model), BF16),
            jax.ShapeDtypeStruct((tok, model), BF16),
            jax.ShapeDtypeStruct(gate_weights.shape[::-1], F32),
            jax.ShapeDtypeStruct((exp_dev, quarter, ff), BF16),
            jax.ShapeDtypeStruct((exp_dev, quarter, ff), BF16),
            jax.ShapeDtypeStruct((exp_dev, ff, quarter), BF16),
        ),
        in_specs=[hbm] * 5 + [vmem] * 2,
        out_specs=[vmem] * 6,
        scratch_shapes=[
            pltpu.VMEM((rows, model), BF16),
            pltpu.VMEM((rows, model), BF16),
            pltpu.VMEM((exp_dev, model, ff), BF16),
            pltpu.VMEM((exp_dev, model, ff), BF16),
            pltpu.VMEM((mids, model), BF16),
            pltpu.VMEM((rows, model), BF16),
            pltpu.VMEM((rows, model), BF16),
            pltpu.VMEM((rows, 2 * mids), BF16),
            pltpu.VMEM((rows, mids), BF16),
            pltpu.VMEM((model, 2 * mids), BF16),
            pltpu.VMEM((dps, mids, quarter), BF16),
            pltpu.VMEM((2, 7, tok, model), BF16),
            pltpu.VMEM((2, quarter, 2 * mids), BF16),
            pltpu.VMEM((2, mids, quarter), BF16),
            pltpu.VMEM((quarter, 2 * mids), BF16),
            pltpu.VMEM((mids, quarter), BF16),
            pltpu.VMEM((owners, 8, 128), F32),
            pltpu.VMEM((owners, 8, 128), F32),
            pltpu.VMEM((exp_dev, rows, 128), F32),
            pltpu.VMEM((exp_dev, rows, 128), F32),
            pltpu.VMEM((owners, 8, 128), F32),
            pltpu.VMEM((owners, 8, 128), F32),
            dma((5,)),
            dma((2, 14)),
            dma((2, 14)),
            dma((2, 7)),
            dma((2, 7)),
            dma((2, 8)),
            dma((2, 8)),
            dma((6,)),
            dma((6,)),
        ],
        compiler_params=pltpu.CompilerParams(
            collective_id=0, has_side_effects=True, vmem_limit_bytes=67_043_328
        ),
        name="moe_layer",
    )(tokens, grad_out, w_gate, w_up, w_down.reshape(mids, model), expert_ids.T, gate_weights.T)
    out = pl.pallas_call(
        hand_over,
        out_shape=tuple(jax.ShapeDtypeStruct(v.shape, v.dtype) for v in out),
        in_specs=[hbm] * 6,
        out_specs=[hbm] * 6,
        scratch_shapes=[pltpu.VMEM(v.shape, v.dtype) for v in out] + [dma((2, 6))],
        compiler_params=pltpu.CompilerParams(vmem_limit_bytes=67_043_328),
        name="hand_over",
    )(*out)
    return (out[0], out[1], out[2].T, *out[3:])


def solution(mesh):
    in_specs = (
        P(("dp", "expert"), None),
        P(("dp", "expert"), None),
        P(("dp", "expert"), None),
        P(("dp", "expert"), None),
        P("expert", None, None),
        P("expert", None, None),
        P("expert", None, None),
    )
    out_specs = (
        P(("dp", "expert"), None),
        P(("dp", "expert"), None),
        P(("dp", "expert"), None),
        P("expert", "dp", None),
        P("expert", "dp", None),
        P("expert", None, "dp"),
    )
    return jax.shard_map(local, mesh=mesh, in_specs=in_specs, out_specs=out_specs, check_vma=False)
```

```python
import functools

import jax
import jax.numpy as jnp
from jax import lax
from jax.experimental import pallas as pl
from jax.experimental.pallas import tpu as pltpu
from jax.sharding import PartitionSpec as P

BF16 = jnp.bfloat16
F32 = jnp.float32
MESH = pl.DeviceIdType.MESH
NN = (((1,), (0,)), ((), ()))
NT = (((1,), (1,)), ((), ()))
TN = (((0,), (0,)), ((), ()))


def dot(spec, a, b):
    return jnp.einsum(spec, a, b, preferred_element_type=F32)


def mm(a, b, dims):
    return lax.dot_general(a, b, dims, preferred_element_type=F32)


def local_wide(tokens, expert_ids, gate_weights, grad_out, w_gate, w_up, w_down):
    tok_dev, model_dim = tokens.shape
    exp_dev = w_gate.shape[0]
    owners = lax.axis_size("expert")
    experts = exp_dev * owners
    chosen = expert_ids[:, :, None] == jnp.arange(experts, dtype=jnp.int32)
    gate_of = jnp.sum(jnp.where(chosen, gate_weights[:, :, None], 0.0), axis=1)
    gates = lax.all_to_all(
        gate_of.reshape(tok_dev, owners, exp_dev).transpose(1, 2, 0), "expert", 0, 0, tiled=True
    )
    gates = gates.transpose(1, 0, 2).reshape(exp_dev, owners * tok_dev, 1)
    rows = lax.all_gather(tokens, "expert", axis=0, tiled=True)
    grads = lax.all_gather(grad_out, "expert", axis=0, tiled=True)
    gate_pre = dot("td,edf->etf", rows, w_gate)
    up_pre = dot("td,edf->etf", rows, w_up)
    d_mid = dot("td,efd->etf", grads, w_down)
    sigma = jax.nn.sigmoid(gate_pre)
    hidden = gate_pre * sigma * up_pre
    d_gate_sum = jnp.sum(hidden * d_mid, axis=2)
    d_hidden = gates * d_mid
    scaled_hidden = (gates * hidden).astype(BF16)
    d_up = (d_hidden * gate_pre * sigma).astype(BF16)
    d_gate = (d_hidden * up_pre * sigma * (1.0 + gate_pre * (1.0 - sigma))).astype(BF16)
    mixed = dot("etf,efd->td", scaled_hidden, w_down).astype(BF16)
    mixed_out = lax.psum_scatter(mixed, "expert", scatter_dimension=0, tiled=True)
    d_rows = (dot("etf,edf->td", d_gate, w_gate) + dot("etf,edf->td", d_up, w_up)).astype(BF16)
    d_tokens = lax.psum_scatter(d_rows, "expert", scatter_dimension=0, tiled=True)
    back = lax.all_to_all(
        d_gate_sum.reshape(exp_dev, owners, tok_dev).transpose(1, 0, 2), "expert", 0, 0, tiled=True
    )
    back = back.reshape(experts, tok_dev).T
    d_gates = jnp.sum(jnp.where(chosen, back[:, None, :], 0.0), axis=2)
    part_gate = dot("td,etf->edf", rows, d_gate).astype(BF16)
    part_up = dot("td,etf->edf", rows, d_up).astype(BF16)
    part_down = dot("etf,td->efd", scaled_hidden, grads).astype(BF16)
    grad_gate = lax.psum_scatter(part_gate, "dp", scatter_dimension=1, tiled=True)
    grad_up = lax.psum_scatter(part_up, "dp", scatter_dimension=1, tiled=True)
    grad_down = lax.psum_scatter(part_down, "dp", scatter_dimension=2, tiled=True)
    return (mixed_out, d_tokens, d_gates, grad_gate, grad_up, grad_down)


CAP_DEV = 48


def slot_of(step):
    if step == 0:
        return 0
    if abs(step) == 4:
        return 1
    return 2 * step if step > 0 else 1 - 2 * step


def step_of(slot):
    if slot == 0:
        return 0
    if slot == 1:
        return 4
    return slot // 2 if slot % 2 == 0 else -(slot // 2)


RETURN_LEFT = (("m", 4), ("r", 3), ("m", 3), ("r", 2), ("m", 2), ("r", 1), ("m", 1))
RETURN_RIGHT = (("r", 4), ("m", -3), ("r", -3), ("m", -2), ("r", -2), ("m", -1), ("r", -1))


def layer_kernel(
    tok_in, grad_in, wg_in, wu_in, wd_in, ids_ref, gw_ref,
    mixed_ref, dtok_ref, dgates_ref, ogate_ref, oup_ref, odown_ref,
    x_all, g_all, wg, wu, wd, parts_m, parts_r, dgu, mid, dwgu, dwd, landed,
    pr_gu, pr_d, xr_gu, xr_d, gsend, grecv, wcol, dcol, dsend, back,
    pick, packed,
    local_sem, ag_send, ag_recv, rs_send, rs_recv, small_send, small_recv, dp_send, dp_recv,
):
    n = 8
    tok, model = tok_in.shape
    exp_dev, ff = wg.shape[0], wg.shape[2]
    half = tok // 2
    few = pick.shape[1]
    quarter = model // 4
    me = lax.axis_index("expert")
    dp = lax.axis_index("dp")
    odd = me % 2
    pos = (me // 2) * (1 - odd) + (n - 1 - me // 2) * odd

    def device_at(q):
        q = (q + 2 * n) % n
        far = q // (n // 2)
        return far * (2 * n - 1 - 2 * q) + (1 - far) * 2 * q

    right, left = device_at(pos + 1), device_at(pos - 1)
    core = dp % 2
    xpos = dp // 2
    partner = xpos * 2 + 1 - core
    across = (1 - xpos) * 2 + core
    sides = (right, left)

    barrier = pltpu.get_barrier_semaphore()
    for k in range(1, n):
        pl.semaphore_signal(
            barrier, inc=1, device_id={"expert": device_at(pos + k)}, device_id_type=MESH
        )
    for other in (partner, across):
        pl.semaphore_signal(barrier, inc=1, device_id={"dp": other}, device_id_type=MESH)

    locals_ = [
        pltpu.make_async_copy(tok_in, x_all.at[pl.ds(0, tok)], local_sem.at[0]),
        pltpu.make_async_copy(grad_in, g_all.at[pl.ds(0, tok)], local_sem.at[1]),
        pltpu.make_async_copy(wg_in, wg, local_sem.at[2]),
        pltpu.make_async_copy(wu_in, wu, local_sem.at[3]),
        pltpu.make_async_copy(wd_in, wd, local_sem.at[4]),
    ]
    for copy in locals_:
        copy.start()
    pl.semaphore_wait(barrier, n + 1)

    def send_to(src, dst, side, index):
        return pltpu.make_async_remote_copy(
            src_ref=src, dst_ref=dst,
            send_sem=ag_send.at[side, index], recv_sem=ag_recv.at[side, index],
            device_id={"expert": sides[side]}, device_id_type=MESH,
        )

    def early(side, index):
        hop, part = index // 2, index % 2
        sign = 1 if side == 0 else -1
        buf, own = ((x_all, tok_in), (g_all, grad_in))[side]
        dst = buf.at[pl.ds(slot_of(sign * (hop + 1)) * tok + part * half, half)]
        if hop == 0:
            src = own.at[pl.ds(part * half, half)]
        else:
            src = buf.at[pl.ds(slot_of(sign * hop) * tok + part * half, half)]
        return send_to(src, dst, side, index)

    def late(side, hop, part):
        if side == 0:
            buf, s, d = g_all, 2 * hop, 2 * hop + 2
        else:
            buf, s, d = x_all, 2 * hop + (hop + 2) // 3, 2 * hop + 3
        return send_to(
            buf.at[pl.ds(s * tok + part * half, half)],
            buf.at[pl.ds(d * tok + part * half, half)],
            side, 8 + 2 * hop + part,
        )

    def packed_copy(side, last):
        landing = (parts_m, parts_r)[side]
        return send_to(
            packed.at[side, last], landing.at[pl.ds((6 + last) * tok, few)], side, 6 + 6 * last
        )

    def squeeze(which, src, base, dst):
        def tile(t, carry):
            cols = pl.ds(pl.multiple_of(t * 512, 512), 512)
            dst[pl.ds(0, few), cols] = mm(
                pick[which], src[pl.ds(base, tok), cols], NN
            ).astype(BF16)
            return carry

        lax.fori_loop(0, model // 512, tile, 0)

    def spread(which, src, base, dst, at):
        def tile(t, carry):
            cols = pl.ds(pl.multiple_of(t * 512, 512), 512)
            dst[pl.ds(at, tok), cols] = mm(
                pick[which], src[pl.ds(base, few), cols], TN
            ).astype(BF16)
            return carry

        lax.fori_loop(0, model // 512, tile, 0)

    def send_packed(side, last):
        if side == 0:
            src, slot, which = ((x_all, 6, 3), (g_all, 4, 4))[last]
        else:
            src, slot, which = ((g_all, 7, 5), (x_all, 5, 6))[last]
        squeeze(which, src, slot * tok, packed.at[side, last])
        packed_copy(side, last).start()

    def take_packed(side, last):
        packed_copy(side, last).wait_recv()
        landing = (parts_m, parts_r)[side]
        if side == 0:
            dst, slot, which = ((x_all, 1, 0), (g_all, 6, 1))[last]
        else:
            dst, slot, which = ((g_all, 1, 0), (x_all, 7, 2))[last]
        spread(which, landing, (6 + last) * tok, dst, slot * tok)

    for part in range(2):
        for side in range(2):
            early(side, part).start()

    line = lax.broadcasted_iota(jnp.int32, (n * 8, tok), 0)
    expert_of_line = jnp.where(line % 8 < exp_dev, (line // 8) * exp_dev + line % 8, -1)
    top = ids_ref.shape[0]
    gates = jnp.zeros((n * 8, tok), F32)
    for k in range(top):
        gates = gates + jnp.where(ids_ref[k : k + 1, :] == expert_of_line, gw_ref[k : k + 1, :], 0.0)
    gsend[...] = gates.reshape(n, 8, tok)

    def gate_copy(k):
        slot = slot_of(k if k <= 4 else k - 8)
        to = device_at(pos + k)
        return pltpu.make_async_remote_copy(
            src_ref=gsend.at[to], dst_ref=grecv.at[slot],
            send_sem=small_send.at[0, slot], recv_sem=small_recv.at[0, slot],
            device_id={"expert": to}, device_id_type=MESH,
        )

    RELAYS = ((3, 4), (2, 3), (-3, -4), (-2, -3))

    def relay_gates(case):
        to, owner = (device_at(pos + k) for k in RELAYS[case])
        return pltpu.make_async_remote_copy(
            src_ref=gsend.at[owner], dst_ref=grecv.at[n + case],
            send_sem=small_send.at[0, n + case], recv_sem=small_recv.at[0, n + case],
            device_id={"expert": to}, device_id_type=MESH,
        )

    for k in range(1, n):
        gate_copy(k).start()
    for case in range(4):
        relay_gates(case).start()
    grecv[0] = gsend[me]
    locals_[0].wait()
    locals_[1].wait()

    for index in range(6):
        for side in range(2):
            early(side, index).wait_recv()
            if index < 4:
                early(side, index + 2).start()
            elif index == 4:
                late(side, 0, 0).start()
            else:
                send_packed(side, 0)
                late(side, 0, 1).start()
        if index == 1:
            for k in range(1, n):
                gate_copy(k).wait_recv()
            for case in range(4):
                relay_gates(case).wait_recv()
            cols = jnp.concatenate(
                [grecv[pl.ds(0, n)].reshape(n * 8, 128), jnp.zeros((128 - n * 8, 128), F32)], axis=0
            )
            cols = jnp.transpose(cols)
            for slot in range(n):
                for e in range(exp_dev):
                    at = slot * 8 + e
                    wcol[e, pl.ds(slot * tok, tok), :] = jnp.broadcast_to(
                        cols[:, at : at + 1], (tok, 128)
                    )
            earlier = (
                lax.broadcasted_iota(jnp.int32, (tok, tok), 0)
                < lax.broadcasted_iota(jnp.int32, (tok, tok), 1)
            ).astype(F32).astype(BF16)
            place = lax.broadcasted_iota(jnp.int32, (few, tok), 0).astype(F32)
            for which, slot in enumerate((1, 6, 7, 8, 9, 10, 11)):
                needed = jnp.max(grecv[slot], axis=0, keepdims=True) > 0.0
                needed = jnp.broadcast_to(jnp.where(needed, 1.0, 0.0), (8, tok))
                rank = mm(needed.astype(BF16), earlier, NN)
                rank = jnp.where(needed > 0.0, rank, -1.0)[0:1, :]
                pick[which] = jnp.where(place == rank, 1.0, 0.0).astype(BF16)
        if index == 3:
            for copy in locals_[2:]:
                copy.wait()
    for side in range(2):
        late(side, 0, 0).wait_recv()
        late(side, 1, 0).start()
    for side in range(2):
        take_packed(side, 0)

    bufs = {"m": parts_m, "r": parts_r}
    orders = (RETURN_RIGHT, RETURN_LEFT)

    def back_copy(side, index):
        kind, step = orders[side][index]
        rows = few if index < 2 else tok
        return pltpu.make_async_remote_copy(
            src_ref=bufs[kind].at[pl.ds(slot_of(step) * tok, rows)],
            dst_ref=landed.at[side, index, pl.ds(0, rows)],
            send_sem=rs_send.at[side, index], recv_sem=rs_recv.at[side, index],
            device_id={"expert": sides[side]}, device_id_type=MESH,
        )

    def return_first(index):
        for side in range(2):
            kind, step = orders[side][index]
            base = slot_of(step) * tok
            which = 0 if index == 0 else 2 - side
            squeeze(which, bufs[kind], base, bufs[kind].at[pl.ds(base, tok)])
            back_copy(side, index).start()

    def stage_one(j):
        rows = pl.ds(pl.multiple_of(j * 2 * tok, 2 * tok), 2 * tok)
        for e in range(exp_dev):
            gate_pre = mm(x_all[rows, :], wg[e], NN)
            up_pre = mm(x_all[rows, :], wu[e], NN)
            d_mid = mm(g_all[rows, :], wd[pl.ds(e * ff, ff), :], NT)
            weight = wcol[e, rows, 0:1]
            sigma = jax.nn.sigmoid(gate_pre)
            hidden = gate_pre * sigma * up_pre
            dots = jnp.sum(hidden * d_mid, axis=1, keepdims=True)
            dcol[e, rows, :] = jnp.broadcast_to(dots, (2 * tok, 128))
            d_hidden = weight * d_mid
            mid[rows, pl.ds(e * ff, ff)] = (weight * hidden).astype(BF16)
            dgu[rows, pl.ds((exp_dev + e) * ff, ff)] = (d_hidden * gate_pre * sigma).astype(BF16)
            dgu[rows, pl.ds(e * ff, ff)] = (
                d_hidden * up_pre * sigma * (1.0 + gate_pre * (1.0 - sigma))
            ).astype(BF16)

    def stage_two(j):
        rows = pl.ds(pl.multiple_of(j * 2 * tok, 2 * tok), 2 * tok)

        def tile(t, carry):
            cols = pl.ds(pl.multiple_of(t * 512, 512), 512)
            parts_m[rows, cols] = mm(mid[rows, :], wd[:, cols], NN).astype(BF16)
            total = None
            for e in range(exp_dev):
                for w, base in ((wg, 0), (wu, exp_dev)):
                    term = mm(dgu[rows, pl.ds((base + e) * ff, ff)], w[e, cols, :], NT)
                    total = term if total is None else total + term
            parts_r[rows, cols] = total.astype(BF16)
            return carry

        lax.fori_loop(0, model // 512, tile, 0)

    def pair(j, carry):
        @pl.when(j == 3)
        def _():
            for side in range(2):
                take_packed(side, 1)

        stage_one(j)

        @pl.when(j == 0)
        def _():
            for side in range(2):
                late(side, 0, 1).wait_recv()
                late(side, 1, 1).start()

        @pl.when(j == 1)
        def _():
            for part in range(2):
                for side in range(2):
                    late(side, 1, part).wait_recv()
            for side in range(2):
                send_packed(side, 1)
            return_first(0)

        stage_two(j)
        return carry

    lax.fori_loop(0, 4, pair, 0)
    return_first(1)

    lane = lax.broadcasted_iota(jnp.int32, (tok, 128), 1)
    stacked = jnp.zeros((tok, 128), F32)
    for slot in range(n):
        for e in range(exp_dev):
            stacked = jnp.where(lane == slot * 8 + e, dcol[e, pl.ds(slot * tok, tok), :], stacked)
    dsend[...] = jnp.transpose(stacked)[: n * 8].reshape(n, 8, 128)

    def dots_copy(slot):
        return pltpu.make_async_remote_copy(
            src_ref=dsend.at[slot], dst_ref=back.at[me],
            send_sem=small_send.at[1, slot], recv_sem=small_recv.at[1, slot],
            device_id={"expert": device_at(pos - step_of(slot))}, device_id_type=MESH,
        )

    for slot in range(1, n):
        dots_copy(slot).start()
    own_dots = pltpu.make_async_copy(dsend.at[0], back.at[me], local_sem.at[0])
    own_dots.start()

    def piece_rows(piece):
        return pl.ds(pl.multiple_of(piece * quarter, quarter), quarter)

    def weight_grads(piece):
        def tile(t, carry):
            base = pl.multiple_of(piece * quarter + t * 256, 256)
            for c in range(2):
                cols = pl.ds(c * exp_dev * ff, exp_dev * ff)
                dwgu[pl.ds(base, 256), cols] = mm(
                    x_all[:, pl.ds(base, 256)], dgu[:, cols], TN
                ).astype(BF16)
            return carry

        lax.fori_loop(0, quarter // 256, tile, 0)

        def tile_down(t, carry):
            at = pl.multiple_of(t * 256, 256)
            dwd[piece, pl.ds(at, 256), :] = mm(
                mid[:, pl.ds(at, 256)], g_all[:, piece_rows(piece)], TN
            ).astype(BF16)
            return carry

        lax.fori_loop(0, exp_dev * ff // 256, tile_down, 0)

    def swap_copies(piece, where):
        return [
            pltpu.make_async_remote_copy(
                src_ref=src, dst_ref=dst, send_sem=dp_send.at[at], recv_sem=dp_recv.at[at],
                device_id={"dp": partner}, device_id_type=MESH,
            )
            for src, dst, at in (
                (dwgu.at[piece_rows(piece)], pr_gu.at[where], 2 * where),
                (dwd.at[piece], pr_d.at[where], 2 * where + 1),
            )
        ]

    far_own, far_partner = (1 - xpos) * 2 + core, (1 - xpos) * 2 + 1 - core
    near_own, near_partner = xpos * 2 + core, xpos * 2 + 1 - core
    far_swap = swap_copies(far_partner, 0)
    near_swap = swap_copies(near_partner, 1)
    far_send = [
        pltpu.make_async_remote_copy(
            src_ref=src, dst_ref=dst, send_sem=dp_send.at[at], recv_sem=dp_recv.at[at],
            device_id={"dp": across}, device_id_type=MESH,
        )
        for src, dst, at in (
            (dwgu.at[piece_rows(far_own)], xr_gu, 4),
            (dwd.at[far_own], xr_d, 5),
        )
    ]

    def return_step(index):
        for side in range(2):
            kind, step = orders[side][index]
            buf, base = bufs[kind], slot_of(step) * tok
            back_copy(side, index - 2).wait_recv()
            if index < 4:
                which = (5, 3)[side] if index == 2 else (6, 4)[side]

                def unpack(t, carry):
                    rows, cols = pl.ds(base, tok), pl.ds(pl.multiple_of(t * 512, 512), 512)
                    got = mm(pick[which], landed[side, index - 2, pl.ds(0, few), cols], TN)
                    buf[rows, cols] = (buf[rows, cols].astype(F32) + got).astype(BF16)
                    return carry

                lax.fori_loop(0, model // 512, unpack, 0)
                back_copy(side, index).start()
                continue

            def add(t, carry):
                rows = pl.ds(pl.multiple_of(base + t * 32, 32), 32)
                got = landed[side, index - 2, pl.ds(pl.multiple_of(t * 32, 32), 32), :]
                buf[rows, :] = (buf[rows, :].astype(F32) + got.astype(F32)).astype(BF16)
                return carry

            lax.fori_loop(0, tok // 32, add, 0)
            back_copy(side, index).start()

    weight_grads(far_partner)
    for copy in far_swap:
        copy.start()
    return_step(2)
    weight_grads(far_own)
    for copy in far_swap:
        copy.wait_recv()

    def add_far(t, carry):
        rows = pl.ds(pl.multiple_of(far_own * quarter + t * 32, 32), 32)
        got = pr_gu[0, pl.ds(pl.multiple_of(t * 32, 32), 32), :]
        dwgu[rows, :] = (dwgu[rows, :].astype(F32) + got.astype(F32)).astype(BF16)
        return carry

    lax.fori_loop(0, quarter // 32, add_far, 0)
    far_send[0].start()

    def add_far_down(t, carry):
        rows = pl.ds(pl.multiple_of(t * 32, 32), 32)
        dwd[far_own, rows, :] = (
            dwd[far_own, rows, :].astype(F32) + pr_d[0, rows, :].astype(F32)
        ).astype(BF16)
        return carry

    lax.fori_loop(0, exp_dev * ff // 32, add_far_down, 0)
    far_send[1].start()
    return_step(3)
    weight_grads(near_partner)
    for copy in near_swap:
        copy.start()
    return_step(4)
    weight_grads(near_own)
    return_step(5)

    own_dots.wait()
    for slot in range(1, n):
        dots_copy(slot).wait_recv()
    got = back[...].reshape(n * 8, tok)
    for k in range(top):
        dgates_ref[k : k + 1, :] = jnp.sum(
            jnp.where(ids_ref[k : k + 1, :] == expert_of_line, got, 0.0), axis=0, keepdims=True
        )
    return_step(6)

    for copy in near_swap:
        copy.wait_recv()
    for copy in far_send:
        copy.wait_recv()

    def final_gu(t, carry):
        rows = pl.ds(pl.multiple_of(t * 32, 32), 32)
        own = pl.ds(pl.multiple_of(near_own * quarter + t * 32, 32), 32)
        total = (
            dwgu[own, :].astype(F32) + pr_gu[1, rows, :].astype(F32) + xr_gu[rows, :].astype(F32)
        ).astype(BF16)
        for e in range(exp_dev):
            ogate_ref[e, rows, :] = total[:, e * ff : (e + 1) * ff]
            oup_ref[e, rows, :] = total[:, (exp_dev + e) * ff : (exp_dev + e + 1) * ff]
        return carry

    lax.fori_loop(0, quarter // 32, final_gu, 0)
    for e in range(exp_dev):
        def final_down(t, carry):
            at = pl.multiple_of(t * 32, 32)
            rows = pl.ds(pl.multiple_of(e * ff + at, 32), 32)
            odown_ref[e, pl.ds(at, 32), :] = (
                dwd[near_own, rows, :].astype(F32)
                + pr_d[1, rows, :].astype(F32)
                + xr_d[rows, :].astype(F32)
            ).astype(BF16)
            return carry

        lax.fori_loop(0, ff // 32, final_down, 0)

    for index in (5, 6):
        for side in range(2):
            back_copy(side, index).wait_recv()
        kind = orders[0][index][0]
        other = orders[1][index][0]
        for side, name in ((0, kind), (1, other)):
            buf, out = bufs[name], {"m": mixed_ref, "r": dtok_ref}[name]

            def close(t, carry):
                rows = pl.ds(pl.multiple_of(t * 32, 32), 32)
                so_far = buf if index == 5 else out
                out[rows, :] = (
                    so_far[rows, :].astype(F32) + landed[side, index, rows, :].astype(F32)
                ).astype(BF16)
                return carry

            lax.fori_loop(0, tok // 32, close, 0)

    for side in range(2):
        for index in range(6):
            early(side, index).wait_send()
        for last in range(2):
            packed_copy(side, last).wait_send()
        for hop in range(2):
            for part in range(2):
                late(side, hop, part).wait_send()
        for index in range(7):
            back_copy(side, index).wait_send()
    for k in range(1, n):
        gate_copy(k).wait_send()
        dots_copy(k).wait_send()
    for case in range(4):
        relay_gates(case).wait_send()
    for copy in far_swap + near_swap + far_send:
        copy.wait_send()


def hand_over(*refs):
    held, sem = refs[12:18], refs[18]
    inward = [pltpu.make_async_copy(refs[i], held[i], sem.at[0, i]) for i in range(6)]
    outward = [pltpu.make_async_copy(held[i], refs[6 + i], sem.at[1, i]) for i in range(6)]
    for copy in inward:
        copy.start()
    for i in range(6):
        inward[i].wait()
        outward[i].start()
    for copy in outward:
        copy.wait()


def local(tokens, expert_ids, gate_weights, grad_out, w_gate, w_up, w_down):
    owners, dps = lax.axis_size("expert"), lax.axis_size("dp")
    if (owners, dps, *w_gate.shape[:1], tokens.shape[0]) != (8, 4, 2, 128):
        return local_wide(tokens, expert_ids, gate_weights, grad_out, w_gate, w_up, w_down)
    tok, model = tokens.shape
    exp_dev, _, ff = w_gate.shape
    rows, mids = owners * tok, exp_dev * ff
    quarter = model // dps
    few = exp_dev * CAP_DEV
    hbm = pl.BlockSpec(memory_space=pl.ANY)
    vmem = pl.BlockSpec(memory_space=pltpu.VMEM)
    dma = pltpu.SemaphoreType.DMA
    out = pl.pallas_call(
        layer_kernel,
        out_shape=(
            jax.ShapeDtypeStruct((tok, model), BF16),
            jax.ShapeDtypeStruct((tok, model), BF16),
            jax.ShapeDtypeStruct(gate_weights.shape[::-1], F32),
            jax.ShapeDtypeStruct((exp_dev, quarter, ff), BF16),
            jax.ShapeDtypeStruct((exp_dev, quarter, ff), BF16),
            jax.ShapeDtypeStruct((exp_dev, ff, quarter), BF16),
        ),
        in_specs=[hbm] * 5 + [vmem] * 2,
        out_specs=[vmem] * 6,
        scratch_shapes=[
            pltpu.VMEM((rows, model), BF16),
            pltpu.VMEM((rows, model), BF16),
            pltpu.VMEM((exp_dev, model, ff), BF16),
            pltpu.VMEM((exp_dev, model, ff), BF16),
            pltpu.VMEM((mids, model), BF16),
            pltpu.VMEM((rows, model), BF16),
            pltpu.VMEM((rows, model), BF16),
            pltpu.VMEM((rows, 2 * mids), BF16),
            pltpu.VMEM((rows, mids), BF16),
            pltpu.VMEM((model, 2 * mids), BF16),
            pltpu.VMEM((dps, mids, quarter), BF16),
            pltpu.VMEM((2, 7, tok, model), BF16),
            pltpu.VMEM((2, quarter, 2 * mids), BF16),
            pltpu.VMEM((2, mids, quarter), BF16),
            pltpu.VMEM((quarter, 2 * mids), BF16),
            pltpu.VMEM((mids, quarter), BF16),
            pltpu.VMEM((owners, 8, 128), F32),
            pltpu.VMEM((owners + 4, 8, 128), F32),
            pltpu.VMEM((exp_dev, rows, 128), F32),
            pltpu.VMEM((exp_dev, rows, 128), F32),
            pltpu.VMEM((owners, 8, 128), F32),
            pltpu.VMEM((owners, 8, 128), F32),
            pltpu.VMEM((7, few, tok), BF16),
            pltpu.VMEM((2, 2, few, model), BF16),
            dma((5,)),
            dma((2, 14)),
            dma((2, 14)),
            dma((2, 7)),
            dma((2, 7)),
            dma((2, 12)),
            dma((2, 12)),
            dma((6,)),
            dma((6,)),
        ],
        compiler_params=pltpu.CompilerParams(
            collective_id=0, has_side_effects=True, vmem_limit_bytes=67_043_328
        ),
        name="moe_layer",
    )(tokens, grad_out, w_gate, w_up, w_down.reshape(mids, model), expert_ids.T, gate_weights.T)
    out = pl.pallas_call(
        hand_over,
        out_shape=tuple(jax.ShapeDtypeStruct(v.shape, v.dtype) for v in out),
        in_specs=[hbm] * 6,
        out_specs=[hbm] * 6,
        scratch_shapes=[pltpu.VMEM(v.shape, v.dtype) for v in out] + [dma((2, 6))],
        compiler_params=pltpu.CompilerParams(vmem_limit_bytes=67_043_328),
        name="hand_over",
    )(*out)
    return (out[0], out[1], out[2].T, *out[3:])


def solution(mesh):
    in_specs = (
        P(("dp", "expert"), None),
        P(("dp", "expert"), None),
        P(("dp", "expert"), None),
        P(("dp", "expert"), None),
        P("expert", None, None),
        P("expert", None, None),
        P("expert", None, None),
    )
    out_specs = (
        P(("dp", "expert"), None),
        P(("dp", "expert"), None),
        P(("dp", "expert"), None),
        P("expert", "dp", None),
        P("expert", "dp", None),
        P("expert", None, "dp"),
    )
    return jax.shard_map(local, mesh=mesh, in_specs=in_specs, out_specs=out_specs, check_vma=False)
```

```python
import functools

import jax
import jax.numpy as jnp
from jax import lax
from jax.experimental import pallas as pl
from jax.experimental.pallas import tpu as pltpu
from jax.sharding import PartitionSpec as P

BF16 = jnp.bfloat16
F32 = jnp.float32
MESH = pl.DeviceIdType.MESH
NN = (((1,), (0,)), ((), ()))
NT = (((1,), (1,)), ((), ()))
TN = (((0,), (0,)), ((), ()))


def dot(spec, a, b):
    return jnp.einsum(spec, a, b, preferred_element_type=F32)


def mm(a, b, dims):
    return lax.dot_general(a, b, dims, preferred_element_type=F32)


def local_wide(tokens, expert_ids, gate_weights, grad_out, w_gate, w_up, w_down):
    tok_dev, model_dim = tokens.shape
    exp_dev = w_gate.shape[0]
    owners = lax.axis_size("expert")
    experts = exp_dev * owners
    chosen = expert_ids[:, :, None] == jnp.arange(experts, dtype=jnp.int32)
    gate_of = jnp.sum(jnp.where(chosen, gate_weights[:, :, None], 0.0), axis=1)
    gates = lax.all_to_all(
        gate_of.reshape(tok_dev, owners, exp_dev).transpose(1, 2, 0), "expert", 0, 0, tiled=True
    )
    gates = gates.transpose(1, 0, 2).reshape(exp_dev, owners * tok_dev, 1)
    rows = lax.all_gather(tokens, "expert", axis=0, tiled=True)
    grads = lax.all_gather(grad_out, "expert", axis=0, tiled=True)
    gate_pre = dot("td,edf->etf", rows, w_gate)
    up_pre = dot("td,edf->etf", rows, w_up)
    d_mid = dot("td,efd->etf", grads, w_down)
    sigma = jax.nn.sigmoid(gate_pre)
    hidden = gate_pre * sigma * up_pre
    d_gate_sum = jnp.sum(hidden * d_mid, axis=2)
    d_hidden = gates * d_mid
    scaled_hidden = (gates * hidden).astype(BF16)
    d_up = (d_hidden * gate_pre * sigma).astype(BF16)
    d_gate = (d_hidden * up_pre * sigma * (1.0 + gate_pre * (1.0 - sigma))).astype(BF16)
    mixed = dot("etf,efd->td", scaled_hidden, w_down).astype(BF16)
    mixed_out = lax.psum_scatter(mixed, "expert", scatter_dimension=0, tiled=True)
    d_rows = (dot("etf,edf->td", d_gate, w_gate) + dot("etf,edf->td", d_up, w_up)).astype(BF16)
    d_tokens = lax.psum_scatter(d_rows, "expert", scatter_dimension=0, tiled=True)
    back = lax.all_to_all(
        d_gate_sum.reshape(exp_dev, owners, tok_dev).transpose(1, 0, 2), "expert", 0, 0, tiled=True
    )
    back = back.reshape(experts, tok_dev).T
    d_gates = jnp.sum(jnp.where(chosen, back[:, None, :], 0.0), axis=2)
    part_gate = dot("td,etf->edf", rows, d_gate).astype(BF16)
    part_up = dot("td,etf->edf", rows, d_up).astype(BF16)
    part_down = dot("etf,td->efd", scaled_hidden, grads).astype(BF16)
    grad_gate = lax.psum_scatter(part_gate, "dp", scatter_dimension=1, tiled=True)
    grad_up = lax.psum_scatter(part_up, "dp", scatter_dimension=1, tiled=True)
    grad_down = lax.psum_scatter(part_down, "dp", scatter_dimension=2, tiled=True)
    return (mixed_out, d_tokens, d_gates, grad_gate, grad_up, grad_down)


CAP_DEV = 48


def slot_of(step):
    if step == 0:
        return 0
    if abs(step) == 4:
        return 1
    return 2 * step if step > 0 else 1 - 2 * step


def step_of(slot):
    if slot == 0:
        return 0
    if slot == 1:
        return 4
    return slot // 2 if slot % 2 == 0 else -(slot // 2)


RETURN_LEFT = (("m", 4), ("r", 3), ("m", 3), ("r", 2), ("m", 2), ("r", 1), ("m", 1))
RETURN_RIGHT = (("r", 4), ("m", -3), ("r", -3), ("m", -2), ("r", -2), ("m", -1), ("r", -1))


def layer_kernel(
    tok_in, grad_in, wg_in, wu_in, wd_in, ids_ref, gw_ref,
    mixed_ref, dtok_ref, dgates_ref, ogate_ref, oup_ref, odown_ref,
    x_all, g_all, wg, wu, wd, parts_m, parts_r, dgu, mid, dwgu, dwd, landed, landed_few,
    pr_gu, pr_d, xr_gu, xr_d, gsend, grecv, wcol, dcol, dsend, back,
    pick, packed, sgate, sup, sdown,
    local_sem, ag_send, ag_recv, rs_send, rs_recv, small_send, small_recv, dp_send, dp_recv,
):
    n = 8
    tok, model = tok_in.shape
    exp_dev, ff = wg.shape[0], wg.shape[2]
    half = tok // 2
    few = pick.shape[1]
    quarter = model // 4
    me = lax.axis_index("expert")
    dp = lax.axis_index("dp")
    odd = me % 2
    pos = (me // 2) * (1 - odd) + (n - 1 - me // 2) * odd

    def device_at(q):
        q = (q + 2 * n) % n
        far = q // (n // 2)
        return far * (2 * n - 1 - 2 * q) + (1 - far) * 2 * q

    right, left = device_at(pos + 1), device_at(pos - 1)
    core = dp % 2
    xpos = dp // 2
    partner = xpos * 2 + 1 - core
    across = (1 - xpos) * 2 + core
    sides = (right, left)

    barrier = pltpu.get_barrier_semaphore()
    for k in range(1, n):
        pl.semaphore_signal(
            barrier, inc=1, device_id={"expert": device_at(pos + k)}, device_id_type=MESH
        )
    for other in (partner, across):
        pl.semaphore_signal(barrier, inc=1, device_id={"dp": other}, device_id_type=MESH)

    locals_ = [
        pltpu.make_async_copy(tok_in, x_all.at[pl.ds(0, tok)], local_sem.at[0]),
        pltpu.make_async_copy(grad_in, g_all.at[pl.ds(0, tok)], local_sem.at[1]),
        pltpu.make_async_copy(wg_in, wg, local_sem.at[2]),
        pltpu.make_async_copy(wu_in, wu, local_sem.at[3]),
        pltpu.make_async_copy(wd_in, wd, local_sem.at[4]),
    ]
    for copy in locals_:
        copy.start()
    pl.semaphore_wait(barrier, n + 1)

    def send_to(src, dst, side, index):
        return pltpu.make_async_remote_copy(
            src_ref=src, dst_ref=dst,
            send_sem=ag_send.at[side, index], recv_sem=ag_recv.at[side, index],
            device_id={"expert": sides[side]}, device_id_type=MESH,
        )

    def early(side, index):
        hop, part = index // 2, index % 2
        sign = 1 if side == 0 else -1
        buf, own = ((x_all, tok_in), (g_all, grad_in))[side]
        dst = buf.at[pl.ds(slot_of(sign * (hop + 1)) * tok + part * half, half)]
        if hop == 0:
            src = own.at[pl.ds(part * half, half)]
        else:
            src = buf.at[pl.ds(slot_of(sign * hop) * tok + part * half, half)]
        return send_to(src, dst, side, index)

    def late(side, hop, part):
        if side == 0:
            buf, s, d = g_all, 2 * hop, 2 * hop + 2
        else:
            buf, s, d = x_all, 2 * hop + (hop + 2) // 3, 2 * hop + 3
        return send_to(
            buf.at[pl.ds(s * tok + part * half, half)],
            buf.at[pl.ds(d * tok + part * half, half)],
            side, 8 + 2 * hop + part,
        )

    def packed_copy(side, last):
        landing = (parts_m, parts_r)[side]
        return send_to(
            packed.at[side, last], landing.at[pl.ds((6 + last) * tok, few)], side, 6 + 6 * last
        )

    def squeeze(which, src, base, dst):
        def tile(t, carry):
            cols = pl.ds(pl.multiple_of(t * 512, 512), 512)
            dst[pl.ds(0, few), cols] = mm(
                pick[which], src[pl.ds(base, tok), cols], NN
            ).astype(BF16)
            return carry

        lax.fori_loop(0, model // 512, tile, 0)

    def spread(which, src, base, dst, at):
        def tile(t, carry):
            cols = pl.ds(pl.multiple_of(t * 512, 512), 512)
            dst[pl.ds(at, tok), cols] = mm(
                pick[which], src[pl.ds(base, few), cols], TN
            ).astype(BF16)
            return carry

        lax.fori_loop(0, model // 512, tile, 0)

    def pack_last(side, last):
        if side == 0:
            src, slot, which = ((x_all, 6, 3), (g_all, 4, 4))[last]
        else:
            src, slot, which = ((g_all, 7, 5), (x_all, 5, 6))[last]
        squeeze(which, src, slot * tok, packed.at[side, last])

    def take_packed(side, last):
        packed_copy(side, last).wait_recv()
        landing = (parts_m, parts_r)[side]
        if side == 0:
            dst, slot, which = ((x_all, 1, 0), (g_all, 6, 1))[last]
        else:
            dst, slot, which = ((g_all, 1, 0), (x_all, 7, 2))[last]
        spread(which, landing, (6 + last) * tok, dst, slot * tok)

    for part in range(2):
        for side in range(2):
            early(side, part).start()

    line = lax.broadcasted_iota(jnp.int32, (n * 8, tok), 0)
    expert_of_line = jnp.where(line % 8 < exp_dev, (line // 8) * exp_dev + line % 8, -1)
    top = ids_ref.shape[0]
    gates = jnp.zeros((n * 8, tok), F32)
    for k in range(top):
        gates = gates + jnp.where(ids_ref[k : k + 1, :] == expert_of_line, gw_ref[k : k + 1, :], 0.0)
    gsend[...] = gates.reshape(n, 8, tok)

    def gate_copy(k):
        slot = slot_of(k if k <= 4 else k - 8)
        to = device_at(pos + k)
        return pltpu.make_async_remote_copy(
            src_ref=gsend.at[to], dst_ref=grecv.at[slot],
            send_sem=small_send.at[0, slot], recv_sem=small_recv.at[0, slot],
            device_id={"expert": to}, device_id_type=MESH,
        )

    RELAYS = ((3, 4), (2, 3), (-3, -4), (-2, -3))

    def relay_gates(case):
        to, owner = (device_at(pos + k) for k in RELAYS[case])
        return pltpu.make_async_remote_copy(
            src_ref=gsend.at[owner], dst_ref=grecv.at[n + case],
            send_sem=small_send.at[0, n + case], recv_sem=small_recv.at[0, n + case],
            device_id={"expert": to}, device_id_type=MESH,
        )

    for k in range(1, n):
        gate_copy(k).start()
    for case in range(4):
        relay_gates(case).start()
    grecv[0] = gsend[me]
    locals_[0].wait()
    locals_[1].wait()

    def stage_one(base, size):
        rows = pl.ds(base, size)
        for e in range(exp_dev):
            gate_pre = mm(x_all[rows, :], wg[e], NN)
            up_pre = mm(x_all[rows, :], wu[e], NN)
            d_mid = mm(g_all[rows, :], wd[pl.ds(e * ff, ff), :], NT)
            weight = wcol[e, rows, 0:1]
            sigma = jax.nn.sigmoid(gate_pre)
            hidden = gate_pre * sigma * up_pre
            dots = jnp.sum(hidden * d_mid, axis=1, keepdims=True)
            dcol[e, rows, :] = jnp.broadcast_to(dots, (size, 128))
            d_hidden = weight * d_mid
            mid[rows, pl.ds(e * ff, ff)] = (weight * hidden).astype(BF16)
            dgu[rows, pl.ds((exp_dev + e) * ff, ff)] = (d_hidden * gate_pre * sigma).astype(BF16)
            dgu[rows, pl.ds(e * ff, ff)] = (
                d_hidden * up_pre * sigma * (1.0 + gate_pre * (1.0 - sigma))
            ).astype(BF16)

    def stage_two(mixed_base, rows_base, size):
        mixed_rows, grad_rows = pl.ds(mixed_base, size), pl.ds(rows_base, size)

        def tile(t, carry):
            cols = pl.ds(pl.multiple_of(t * 512, 512), 512)
            parts_m[mixed_rows, cols] = mm(mid[mixed_rows, :], wd[:, cols], NN).astype(BF16)
            total = None
            for e in range(exp_dev):
                for w, base in ((wg, 0), (wu, exp_dev)):
                    term = mm(dgu[grad_rows, pl.ds((base + e) * ff, ff)], w[e, cols, :], NT)
                    total = term if total is None else total + term
            parts_r[grad_rows, cols] = total.astype(BF16)
            return carry

        lax.fori_loop(0, model // 512, tile, 0)

    for index in range(6):
        for side in range(2):
            early(side, index).wait_recv()
            if index < 4:
                early(side, index + 2).start()
            else:
                late(side, 0, index - 4).start()
        if index == 1:
            for k in range(1, n):
                gate_copy(k).wait_recv()
            for case in range(4):
                relay_gates(case).wait_recv()
            cols = jnp.concatenate(
                [grecv[pl.ds(0, n)].reshape(n * 8, 128), jnp.zeros((128 - n * 8, 128), F32)], axis=0
            )
            cols = jnp.transpose(cols)
            for slot in range(n):
                for e in range(exp_dev):
                    at = slot * 8 + e
                    wcol[e, pl.ds(slot * tok, tok), :] = jnp.broadcast_to(
                        cols[:, at : at + 1], (tok, 128)
                    )
            earlier = (
                lax.broadcasted_iota(jnp.int32, (tok, tok), 0)
                < lax.broadcasted_iota(jnp.int32, (tok, tok), 1)
            ).astype(F32).astype(BF16)
            place = lax.broadcasted_iota(jnp.int32, (few, tok), 0).astype(F32)
            for which, slot in enumerate((1, 6, 7, 8, 9, 10, 11)):
                needed = jnp.max(grecv[slot], axis=0, keepdims=True) > 0.0
                needed = jnp.broadcast_to(jnp.where(needed, 1.0, 0.0), (8, tok))
                rank = mm(needed.astype(BF16), earlier, NN)
                rank = jnp.where(needed > 0.0, rank, -1.0)[0:1, :]
                pick[which] = jnp.where(place == rank, 1.0, 0.0).astype(BF16)
        if index == 2:
            for copy in locals_[2:]:
                copy.wait()
            stage_one(0, tok)
        if index == 3:
            stage_two(0, 0, tok)
    for side in range(2):
        pack_last(side, 0)
    for part in range(2):
        for side in range(2):
            late(side, 0, part).wait_recv()
            late(side, 1, part).start()
    for side in range(2):
        packed_copy(side, 0).start()

    bufs = {"m": parts_m, "r": parts_r}
    orders = (RETURN_RIGHT, RETURN_LEFT)

    def back_copy(side, index):
        kind, step = orders[side][index]
        rows = few if index < 2 else tok
        return pltpu.make_async_remote_copy(
            src_ref=bufs[kind].at[pl.ds(slot_of(step) * tok, rows)],
            dst_ref=landed_few.at[side, index] if index < 2 else landed.at[side, index - 2],
            send_sem=rs_send.at[side, index], recv_sem=rs_recv.at[side, index],
            device_id={"expert": sides[side]}, device_id_type=MESH,
        )

    def return_first(index):
        for side in range(2):
            kind, step = orders[side][index]
            base = slot_of(step) * tok
            which = 0 if index == 0 else 2 - side
            squeeze(which, bufs[kind], base, bufs[kind].at[pl.ds(base, tok)])
            back_copy(side, index).start()

    def pair(j, carry):
        base = pl.multiple_of(j * 2 * tok, 2 * tok)

        @pl.when(j == 2)
        def _():
            for part in range(2):
                for side in range(2):
                    late(side, 1, part).wait_recv()
            for side in range(2):
                pack_last(side, 1)
                packed_copy(side, 1).start()

        @pl.when(j == 3)
        def _():
            for side in range(2):
                take_packed(side, 0)
            stage_one(tok, tok)
            stage_two(tok, tok, tok)
            return_first(0)
            for side in range(2):
                take_packed(side, 1)

        stage_one(base, 2 * tok)

        @pl.when(j < 3)
        def _():
            stage_two(base, base, 2 * tok)

        return carry

    lax.fori_loop(1, 4, pair, 0)
    stage_two(7 * tok, 6 * tok, tok)
    return_first(1)
    stage_two(6 * tok, 7 * tok, tok)

    lane = lax.broadcasted_iota(jnp.int32, (tok, 128), 1)
    stacked = jnp.zeros((tok, 128), F32)
    for slot in range(n):
        for e in range(exp_dev):
            stacked = jnp.where(lane == slot * 8 + e, dcol[e, pl.ds(slot * tok, tok), :], stacked)
    dsend[...] = jnp.transpose(stacked)[: n * 8].reshape(n, 8, 128)

    def dots_copy(slot):
        return pltpu.make_async_remote_copy(
            src_ref=dsend.at[slot], dst_ref=back.at[me],
            send_sem=small_send.at[1, slot], recv_sem=small_recv.at[1, slot],
            device_id={"expert": device_at(pos - step_of(slot))}, device_id_type=MESH,
        )

    for slot in range(1, n):
        dots_copy(slot).start()
    own_dots = pltpu.make_async_copy(dsend.at[0], back.at[me], local_sem.at[0])
    own_dots.start()

    def piece_rows(piece):
        return pl.ds(pl.multiple_of(piece * quarter, quarter), quarter)

    def weight_grads(piece):
        def tile(t, carry):
            base = pl.multiple_of(piece * quarter + t * 256, 256)
            for c in range(2):
                cols = pl.ds(c * exp_dev * ff, exp_dev * ff)
                dwgu[pl.ds(base, 256), cols] = mm(
                    x_all[:, pl.ds(base, 256)], dgu[:, cols], TN
                ).astype(BF16)
            return carry

        lax.fori_loop(0, quarter // 256, tile, 0)

        def tile_down(t, carry):
            at = pl.multiple_of(t * 256, 256)
            dwd[piece, pl.ds(at, 256), :] = mm(
                mid[:, pl.ds(at, 256)], g_all[:, piece_rows(piece)], TN
            ).astype(BF16)
            return carry

        lax.fori_loop(0, exp_dev * ff // 256, tile_down, 0)

    def swap_copies(piece, where):
        return [
            pltpu.make_async_remote_copy(
                src_ref=src, dst_ref=dst, send_sem=dp_send.at[at], recv_sem=dp_recv.at[at],
                device_id={"dp": partner}, device_id_type=MESH,
            )
            for src, dst, at in (
                (dwgu.at[piece_rows(piece)], pr_gu.at[where], 2 * where),
                (dwd.at[piece], pr_d.at[where], 2 * where + 1),
            )
        ]

    far_own, far_partner = (1 - xpos) * 2 + core, (1 - xpos) * 2 + 1 - core
    near_own, near_partner = xpos * 2 + core, xpos * 2 + 1 - core
    far_swap = swap_copies(far_partner, 0)
    near_swap = swap_copies(near_partner, 1)
    far_send = [
        pltpu.make_async_remote_copy(
            src_ref=src, dst_ref=dst, send_sem=dp_send.at[at], recv_sem=dp_recv.at[at],
            device_id={"dp": across}, device_id_type=MESH,
        )
        for src, dst, at in (
            (dwgu.at[piece_rows(far_own)], xr_gu, 4),
            (dwd.at[far_own], xr_d, 5),
        )
    ]

    def return_step(index):
        for side in range(2):
            kind, step = orders[side][index]
            buf, base = bufs[kind], slot_of(step) * tok
            back_copy(side, index - 2).wait_recv()
            if index < 4:
                which = (5, 3)[side] if index == 2 else (6, 4)[side]

                def unpack(t, carry):
                    rows, cols = pl.ds(base, tok), pl.ds(pl.multiple_of(t * 512, 512), 512)
                    got = mm(pick[which], landed_few[side, index - 2, :, cols], TN)
                    buf[rows, cols] = (buf[rows, cols].astype(F32) + got).astype(BF16)
                    return carry

                lax.fori_loop(0, model // 512, unpack, 0)
                back_copy(side, index).start()
                continue

            def add(t, carry):
                rows = pl.ds(pl.multiple_of(base + t * 32, 32), 32)
                got = landed[side, index - 4, pl.ds(pl.multiple_of(t * 32, 32), 32), :]
                buf[rows, :] = (buf[rows, :].astype(F32) + got.astype(F32)).astype(BF16)
                return carry

            lax.fori_loop(0, tok // 32, add, 0)
            back_copy(side, index).start()

    weight_grads(far_partner)
    for copy in far_swap:
        copy.start()
    return_step(2)
    weight_grads(far_own)
    for copy in far_swap:
        copy.wait_recv()

    def add_far(t, carry):
        rows = pl.ds(pl.multiple_of(far_own * quarter + t * 32, 32), 32)
        got = pr_gu[0, pl.ds(pl.multiple_of(t * 32, 32), 32), :]
        dwgu[rows, :] = (dwgu[rows, :].astype(F32) + got.astype(F32)).astype(BF16)
        return carry

    lax.fori_loop(0, quarter // 32, add_far, 0)
    far_send[0].start()

    def add_far_down(t, carry):
        rows = pl.ds(pl.multiple_of(t * 32, 32), 32)
        dwd[far_own, rows, :] = (
            dwd[far_own, rows, :].astype(F32) + pr_d[0, rows, :].astype(F32)
        ).astype(BF16)
        return carry

    lax.fori_loop(0, exp_dev * ff // 32, add_far_down, 0)
    far_send[1].start()
    return_step(3)
    weight_grads(near_partner)
    for copy in near_swap:
        copy.start()
    return_step(4)
    weight_grads(near_own)
    return_step(5)

    own_dots.wait()
    for slot in range(1, n):
        dots_copy(slot).wait_recv()
    got = back[...].reshape(n * 8, tok)
    for k in range(top):
        dgates_ref[k : k + 1, :] = jnp.sum(
            jnp.where(ids_ref[k : k + 1, :] == expert_of_line, got, 0.0), axis=0, keepdims=True
        )
    return_step(6)

    for copy in near_swap:
        copy.wait_recv()
    for copy in far_send:
        copy.wait_recv()

    def final_gu(t, carry):
        rows = pl.ds(pl.multiple_of(t * 32, 32), 32)
        own = pl.ds(pl.multiple_of(near_own * quarter + t * 32, 32), 32)
        total = (
            dwgu[own, :].astype(F32) + pr_gu[1, rows, :].astype(F32) + xr_gu[rows, :].astype(F32)
        ).astype(BF16)
        for e in range(exp_dev):
            sgate[e, rows, :] = total[:, e * ff : (e + 1) * ff]
            sup[e, rows, :] = total[:, (exp_dev + e) * ff : (exp_dev + e + 1) * ff]
        return carry

    lax.fori_loop(0, quarter // 32, final_gu, 0)
    for e in range(exp_dev):
        def final_down(t, carry):
            at = pl.multiple_of(t * 32, 32)
            rows = pl.ds(pl.multiple_of(e * ff + at, 32), 32)
            sdown[e, pl.ds(at, 32), :] = (
                dwd[near_own, rows, :].astype(F32)
                + pr_d[1, rows, :].astype(F32)
                + xr_d[rows, :].astype(F32)
            ).astype(BF16)
            return carry

        lax.fori_loop(0, ff // 32, final_down, 0)

    leaving = [
        pltpu.make_async_copy(sgate, ogate_ref, local_sem.at[1]),
        pltpu.make_async_copy(sup, oup_ref, local_sem.at[2]),
        pltpu.make_async_copy(sdown, odown_ref, local_sem.at[3]),
    ]
    for copy in leaving:
        copy.start()

    for index in (5, 6):
        for side in range(2):
            back_copy(side, index).wait_recv()
        kind = orders[0][index][0]
        other = orders[1][index][0]
        for side, name in ((0, kind), (1, other)):
            buf, out = bufs[name], {"m": mixed_ref, "r": dtok_ref}[name]

            def close(t, carry):
                rows = pl.ds(pl.multiple_of(t * 32, 32), 32)
                so_far = buf if index == 5 else out
                out[rows, :] = (
                    so_far[rows, :].astype(F32) + landed[side, index - 2, rows, :].astype(F32)
                ).astype(BF16)
                return carry

            lax.fori_loop(0, tok // 32, close, 0)

    for side in range(2):
        for index in range(6):
            early(side, index).wait_send()
        for last in range(2):
            packed_copy(side, last).wait_send()
        for hop in range(2):
            for part in range(2):
                late(side, hop, part).wait_send()
        for index in range(7):
            back_copy(side, index).wait_send()
    for k in range(1, n):
        gate_copy(k).wait_send()
        dots_copy(k).wait_send()
    for case in range(4):
        relay_gates(case).wait_send()
    for copy in leaving:
        copy.wait()
    for copy in far_swap + near_swap + far_send:
        copy.wait_send()


def hand_over(*refs):
    held, sem = refs[12:18], refs[18]
    inward = [pltpu.make_async_copy(refs[i], held[i], sem.at[0, i]) for i in range(6)]
    outward = [pltpu.make_async_copy(held[i], refs[6 + i], sem.at[1, i]) for i in range(6)]
    for copy in inward:
        copy.start()
    for i in range(6):
        inward[i].wait()
        outward[i].start()
    for copy in outward:
        copy.wait()


def local(tokens, expert_ids, gate_weights, grad_out, w_gate, w_up, w_down):
    owners, dps = lax.axis_size("expert"), lax.axis_size("dp")
    if (owners, dps, *w_gate.shape[:1], tokens.shape[0]) != (8, 4, 2, 128):
        return local_wide(tokens, expert_ids, gate_weights, grad_out, w_gate, w_up, w_down)
    tok, model = tokens.shape
    exp_dev, _, ff = w_gate.shape
    rows, mids = owners * tok, exp_dev * ff
    quarter = model // dps
    few = exp_dev * CAP_DEV
    hbm = pl.BlockSpec(memory_space=pl.ANY)
    vmem = pl.BlockSpec(memory_space=pltpu.VMEM)
    dma = pltpu.SemaphoreType.DMA
    out = pl.pallas_call(
        layer_kernel,
        out_shape=(
            jax.ShapeDtypeStruct((tok, model), BF16),
            jax.ShapeDtypeStruct((tok, model), BF16),
            jax.ShapeDtypeStruct(gate_weights.shape[::-1], F32),
            jax.ShapeDtypeStruct((exp_dev, quarter, ff), BF16),
            jax.ShapeDtypeStruct((exp_dev, quarter, ff), BF16),
            jax.ShapeDtypeStruct((exp_dev, ff, quarter), BF16),
        ),
        in_specs=[hbm] * 5 + [vmem] * 2,
        out_specs=[vmem] * 3 + [hbm] * 3,
        scratch_shapes=[
            pltpu.VMEM((rows, model), BF16),
            pltpu.VMEM((rows, model), BF16),
            pltpu.VMEM((exp_dev, model, ff), BF16),
            pltpu.VMEM((exp_dev, model, ff), BF16),
            pltpu.VMEM((mids, model), BF16),
            pltpu.VMEM((rows, model), BF16),
            pltpu.VMEM((rows, model), BF16),
            pltpu.VMEM((rows, 2 * mids), BF16),
            pltpu.VMEM((rows, mids), BF16),
            pltpu.VMEM((model, 2 * mids), BF16),
            pltpu.VMEM((dps, mids, quarter), BF16),
            pltpu.VMEM((2, 5, tok, model), BF16),
            pltpu.VMEM((2, 2, few, model), BF16),
            pltpu.VMEM((2, quarter, 2 * mids), BF16),
            pltpu.VMEM((2, mids, quarter), BF16),
            pltpu.VMEM((quarter, 2 * mids), BF16),
            pltpu.VMEM((mids, quarter), BF16),
            pltpu.VMEM((owners, 8, 128), F32),
            pltpu.VMEM((owners + 4, 8, 128), F32),
            pltpu.VMEM((exp_dev, rows, 128), F32),
            pltpu.VMEM((exp_dev, rows, 128), F32),
            pltpu.VMEM((owners, 8, 128), F32),
            pltpu.VMEM((owners, 8, 128), F32),
            pltpu.VMEM((7, few, tok), BF16),
            pltpu.VMEM((2, 2, few, model), BF16),
            pltpu.VMEM((exp_dev, quarter, ff), BF16),
            pltpu.VMEM((exp_dev, quarter, ff), BF16),
            pltpu.VMEM((exp_dev, ff, quarter), BF16),
            dma((5,)),
            dma((2, 14)),
            dma((2, 14)),
            dma((2, 7)),
            dma((2, 7)),
            dma((2, 12)),
            dma((2, 12)),
            dma((6,)),
            dma((6,)),
        ],
        compiler_params=pltpu.CompilerParams(
            collective_id=0, has_side_effects=True, vmem_limit_bytes=67_043_328
        ),
        name="moe_layer",
    )(tokens, grad_out, w_gate, w_up, w_down.reshape(mids, model), expert_ids.T, gate_weights.T)
    out = pl.pallas_call(
        hand_over,
        out_shape=tuple(jax.ShapeDtypeStruct(v.shape, v.dtype) for v in out),
        in_specs=[hbm] * 6,
        out_specs=[hbm] * 6,
        scratch_shapes=[pltpu.VMEM(v.shape, v.dtype) for v in out] + [dma((2, 6))],
        compiler_params=pltpu.CompilerParams(vmem_limit_bytes=67_043_328),
        name="hand_over",
    )(*out)
    return (out[0], out[1], out[2].T, *out[3:])


def solution(mesh):
    in_specs = (
        P(("dp", "expert"), None),
        P(("dp", "expert"), None),
        P(("dp", "expert"), None),
        P(("dp", "expert"), None),
        P("expert", None, None),
        P("expert", None, None),
        P("expert", None, None),
    )
    out_specs = (
        P(("dp", "expert"), None),
        P(("dp", "expert"), None),
        P(("dp", "expert"), None),
        P("expert", "dp", None),
        P("expert", "dp", None),
        P("expert", None, "dp"),
    )
    return jax.shard_map(local, mesh=mesh, in_specs=in_specs, out_specs=out_specs, check_vma=False)
```

```python
import functools

import jax
import jax.numpy as jnp
from jax import lax
from jax.experimental import pallas as pl
from jax.experimental.pallas import tpu as pltpu
from jax.sharding import PartitionSpec as P

BF16 = jnp.bfloat16
F32 = jnp.float32
MESH = pl.DeviceIdType.MESH
NN = (((1,), (0,)), ((), ()))
NT = (((1,), (1,)), ((), ()))
TN = (((0,), (0,)), ((), ()))


def dot(spec, a, b):
    return jnp.einsum(spec, a, b, preferred_element_type=F32)


def mm(a, b, dims):
    return lax.dot_general(a, b, dims, preferred_element_type=F32)


def local_wide(tokens, expert_ids, gate_weights, grad_out, w_gate, w_up, w_down):
    tok_dev, model_dim = tokens.shape
    exp_dev = w_gate.shape[0]
    owners = lax.axis_size("expert")
    experts = exp_dev * owners
    chosen = expert_ids[:, :, None] == jnp.arange(experts, dtype=jnp.int32)
    gate_of = jnp.sum(jnp.where(chosen, gate_weights[:, :, None], 0.0), axis=1)
    gates = lax.all_to_all(
        gate_of.reshape(tok_dev, owners, exp_dev).transpose(1, 2, 0), "expert", 0, 0, tiled=True
    )
    gates = gates.transpose(1, 0, 2).reshape(exp_dev, owners * tok_dev, 1)
    rows = lax.all_gather(tokens, "expert", axis=0, tiled=True)
    grads = lax.all_gather(grad_out, "expert", axis=0, tiled=True)
    gate_pre = dot("td,edf->etf", rows, w_gate)
    up_pre = dot("td,edf->etf", rows, w_up)
    d_mid = dot("td,efd->etf", grads, w_down)
    sigma = jax.nn.sigmoid(gate_pre)
    hidden = gate_pre * sigma * up_pre
    d_gate_sum = jnp.sum(hidden * d_mid, axis=2)
    d_hidden = gates * d_mid
    scaled_hidden = (gates * hidden).astype(BF16)
    d_up = (d_hidden * gate_pre * sigma).astype(BF16)
    d_gate = (d_hidden * up_pre * sigma * (1.0 + gate_pre * (1.0 - sigma))).astype(BF16)
    mixed = dot("etf,efd->td", scaled_hidden, w_down).astype(BF16)
    mixed_out = lax.psum_scatter(mixed, "expert", scatter_dimension=0, tiled=True)
    d_rows = (dot("etf,edf->td", d_gate, w_gate) + dot("etf,edf->td", d_up, w_up)).astype(BF16)
    d_tokens = lax.psum_scatter(d_rows, "expert", scatter_dimension=0, tiled=True)
    back = lax.all_to_all(
        d_gate_sum.reshape(exp_dev, owners, tok_dev).transpose(1, 0, 2), "expert", 0, 0, tiled=True
    )
    back = back.reshape(experts, tok_dev).T
    d_gates = jnp.sum(jnp.where(chosen, back[:, None, :], 0.0), axis=2)
    part_gate = dot("td,etf->edf", rows, d_gate).astype(BF16)
    part_up = dot("td,etf->edf", rows, d_up).astype(BF16)
    part_down = dot("etf,td->efd", scaled_hidden, grads).astype(BF16)
    grad_gate = lax.psum_scatter(part_gate, "dp", scatter_dimension=1, tiled=True)
    grad_up = lax.psum_scatter(part_up, "dp", scatter_dimension=1, tiled=True)
    grad_down = lax.psum_scatter(part_down, "dp", scatter_dimension=2, tiled=True)
    return (mixed_out, d_tokens, d_gates, grad_gate, grad_up, grad_down)


CAP_DEV = 48


def slot_of(step):
    if step == 0:
        return 0
    if abs(step) == 4:
        return 1
    return 2 * step if step > 0 else 1 - 2 * step


def step_of(slot):
    if slot == 0:
        return 0
    if slot == 1:
        return 4
    return slot // 2 if slot % 2 == 0 else -(slot // 2)


RETURN_LEFT = (("m", 4), ("r", 3), ("m", 3), ("r", 2), ("m", 2), ("r", 1), ("m", 1))
RETURN_RIGHT = (("r", 4), ("m", -3), ("r", -3), ("m", -2), ("r", -2), ("m", -1), ("r", -1))


def layer_kernel(
    tok_in, grad_in, wg_in, wu_in, wd_in, ids_ref, gw_ref,
    mixed_ref, dtok_ref, dgates_ref, ogate_ref, oup_ref, odown_ref,
    x_all, g_all, wg, wu, wd, parts_m, parts_r, dgu, mid, dwgu, dwd, landed, landed_few,
    pr_gu, pr_d, xr_gu, xr_d, gsend, grecv, wcol, dcol, dsend, back,
    pick, packed, sgate, sup, sdown,
    local_sem, ag_send, ag_recv, rs_send, rs_recv, small_send, small_recv, dp_send, dp_recv,
):
    n = 8
    tok, model = tok_in.shape
    exp_dev, ff = wg.shape[0], wg.shape[2]
    half = tok // 2
    few = pick.shape[1]
    quarter = model // 4
    me = lax.axis_index("expert")
    dp = lax.axis_index("dp")
    odd = me % 2
    pos = (me // 2) * (1 - odd) + (n - 1 - me // 2) * odd

    def device_at(q):
        q = (q + 2 * n) % n
        far = q // (n // 2)
        return far * (2 * n - 1 - 2 * q) + (1 - far) * 2 * q

    right, left = device_at(pos + 1), device_at(pos - 1)
    core = dp % 2
    xpos = dp // 2
    partner = xpos * 2 + 1 - core
    across = (1 - xpos) * 2 + core
    sides = (right, left)

    barrier = pltpu.get_barrier_semaphore()
    for k in range(1, n):
        pl.semaphore_signal(
            barrier, inc=1, device_id={"expert": device_at(pos + k)}, device_id_type=MESH
        )
    for other in (partner, across):
        pl.semaphore_signal(barrier, inc=1, device_id={"dp": other}, device_id_type=MESH)

    locals_ = [
        pltpu.make_async_copy(tok_in, x_all.at[pl.ds(0, tok)], local_sem.at[0]),
        pltpu.make_async_copy(grad_in, g_all.at[pl.ds(0, tok)], local_sem.at[1]),
        pltpu.make_async_copy(wg_in, wg, local_sem.at[2]),
        pltpu.make_async_copy(wu_in, wu, local_sem.at[3]),
        pltpu.make_async_copy(wd_in, wd, local_sem.at[4]),
    ]
    for copy in locals_:
        copy.start()
    pl.semaphore_wait(barrier, n + 1)

    def send_to(src, dst, side, index):
        return pltpu.make_async_remote_copy(
            src_ref=src, dst_ref=dst,
            send_sem=ag_send.at[side, index], recv_sem=ag_recv.at[side, index],
            device_id={"expert": sides[side]}, device_id_type=MESH,
        )

    def early(side, index):
        hop, part = index // 2, index % 2
        sign = 1 if side == 0 else -1
        buf, own = ((x_all, tok_in), (g_all, grad_in))[side]
        dst = buf.at[pl.ds(slot_of(sign * (hop + 1)) * tok + part * half, half)]
        if hop == 0:
            src = own.at[pl.ds(part * half, half)]
        else:
            src = buf.at[pl.ds(slot_of(sign * hop) * tok + part * half, half)]
        return send_to(src, dst, side, index)

    def late(side, hop, part):
        if side == 0:
            buf, s, d = g_all, 2 * hop, 2 * hop + 2
        else:
            buf, s, d = x_all, 2 * hop + (hop + 2) // 3, 2 * hop + 3
        return send_to(
            buf.at[pl.ds(s * tok + part * half, half)],
            buf.at[pl.ds(d * tok + part * half, half)],
            side, 8 + 2 * hop + part,
        )

    def packed_copy(side, last):
        landing = (parts_m, parts_r)[side]
        return send_to(
            packed.at[side, last], landing.at[pl.ds((6 + last) * tok, few)], side, 6 + 6 * last
        )

    def squeeze(which, src, base, dst):
        def tile(t, carry):
            cols = pl.ds(pl.multiple_of(t * 512, 512), 512)
            dst[pl.ds(0, few), cols] = mm(
                pick[which], src[pl.ds(base, tok), cols], NN
            ).astype(BF16)
            return carry

        lax.fori_loop(0, model // 512, tile, 0)

    def spread(which, src, base, dst, at):
        def tile(t, carry):
            cols = pl.ds(pl.multiple_of(t * 512, 512), 512)
            dst[pl.ds(at, tok), cols] = mm(
                pick[which], src[pl.ds(base, few), cols], TN
            ).astype(BF16)
            return carry

        lax.fori_loop(0, model // 512, tile, 0)

    def pack_last(side, last):
        if side == 0:
            src, slot, which = ((x_all, 6, 3), (g_all, 4, 4))[last]
        else:
            src, slot, which = ((g_all, 7, 5), (x_all, 5, 6))[last]
        squeeze(which, src, slot * tok, packed.at[side, last])

    def take_packed(side, last):
        packed_copy(side, last).wait_recv()
        landing = (parts_m, parts_r)[side]
        if side == 0:
            dst, slot, which = ((x_all, 1, 0), (g_all, 6, 1))[last]
        else:
            dst, slot, which = ((g_all, 1, 0), (x_all, 7, 2))[last]
        spread(which, landing, (6 + last) * tok, dst, slot * tok)

    for part in range(2):
        for side in range(2):
            early(side, part).start()

    line = lax.broadcasted_iota(jnp.int32, (n * 8, tok), 0)
    expert_of_line = jnp.where(line % 8 < exp_dev, (line // 8) * exp_dev + line % 8, -1)
    top = ids_ref.shape[0]
    gates = jnp.zeros((n * 8, tok), F32)
    for k in range(top):
        gates = gates + jnp.where(ids_ref[k : k + 1, :] == expert_of_line, gw_ref[k : k + 1, :], 0.0)
    gsend[...] = gates.reshape(n, 8, tok)

    def gate_copy(k):
        slot = slot_of(k if k <= 4 else k - 8)
        to = device_at(pos + k)
        return pltpu.make_async_remote_copy(
            src_ref=gsend.at[to], dst_ref=grecv.at[slot],
            send_sem=small_send.at[0, slot], recv_sem=small_recv.at[0, slot],
            device_id={"expert": to}, device_id_type=MESH,
        )

    RELAYS = ((3, 4), (2, 3), (-3, -4), (-2, -3))

    def relay_gates(case):
        to, owner = (device_at(pos + k) for k in RELAYS[case])
        return pltpu.make_async_remote_copy(
            src_ref=gsend.at[owner], dst_ref=grecv.at[n + case],
            send_sem=small_send.at[0, n + case], recv_sem=small_recv.at[0, n + case],
            device_id={"expert": to}, device_id_type=MESH,
        )

    for k in range(1, n):
        gate_copy(k).start()
    for case in range(4):
        relay_gates(case).start()
    grecv[0] = gsend[me]
    locals_[0].wait()
    locals_[1].wait()

    def stage_one(base, size):
        rows = pl.ds(base, size)
        for e in range(exp_dev):
            gate_pre = mm(x_all[rows, :], wg[e], NN)
            up_pre = mm(x_all[rows, :], wu[e], NN)
            d_mid = mm(g_all[rows, :], wd[pl.ds(e * ff, ff), :], NT)
            weight = wcol[e, rows, 0:1]
            sigma = jax.nn.sigmoid(gate_pre)
            hidden = gate_pre * sigma * up_pre
            dots = jnp.sum(hidden * d_mid, axis=1, keepdims=True)
            dcol[e, rows, :] = jnp.broadcast_to(dots, (size, 128))
            d_hidden = weight * d_mid
            mid[rows, pl.ds(e * ff, ff)] = (weight * hidden).astype(BF16)
            dgu[rows, pl.ds((exp_dev + e) * ff, ff)] = (d_hidden * gate_pre * sigma).astype(BF16)
            dgu[rows, pl.ds(e * ff, ff)] = (
                d_hidden * up_pre * sigma * (1.0 + gate_pre * (1.0 - sigma))
            ).astype(BF16)

    def stage_two(mixed_base, rows_base, size):
        mixed_rows, grad_rows = pl.ds(mixed_base, size), pl.ds(rows_base, size)

        def tile(t, carry):
            cols = pl.ds(pl.multiple_of(t * 512, 512), 512)
            parts_m[mixed_rows, cols] = mm(mid[mixed_rows, :], wd[:, cols], NN).astype(BF16)
            total = None
            for e in range(exp_dev):
                for w, base in ((wg, 0), (wu, exp_dev)):
                    term = mm(dgu[grad_rows, pl.ds((base + e) * ff, ff)], w[e, cols, :], NT)
                    total = term if total is None else total + term
            parts_r[grad_rows, cols] = total.astype(BF16)
            return carry

        lax.fori_loop(0, model // 512, tile, 0)

    for index in range(6):
        for side in range(2):
            early(side, index).wait_recv()
            if index < 4:
                early(side, index + 2).start()
            else:
                late(side, 0, index - 4).start()
        if index == 1:
            for k in range(1, n):
                gate_copy(k).wait_recv()
            for case in range(4):
                relay_gates(case).wait_recv()
            cols = jnp.concatenate(
                [grecv[pl.ds(0, n)].reshape(n * 8, 128), jnp.zeros((128 - n * 8, 128), F32)], axis=0
            )
            cols = jnp.transpose(cols)
            for slot in range(n):
                for e in range(exp_dev):
                    at = slot * 8 + e
                    wcol[e, pl.ds(slot * tok, tok), :] = jnp.broadcast_to(
                        cols[:, at : at + 1], (tok, 128)
                    )
            earlier = (
                lax.broadcasted_iota(jnp.int32, (tok, tok), 0)
                < lax.broadcasted_iota(jnp.int32, (tok, tok), 1)
            ).astype(F32).astype(BF16)
            place = lax.broadcasted_iota(jnp.int32, (few, tok), 0).astype(F32)
            for which, slot in enumerate((1, 6, 7, 8, 9, 10, 11)):
                needed = jnp.max(grecv[slot], axis=0, keepdims=True) > 0.0
                needed = jnp.broadcast_to(jnp.where(needed, 1.0, 0.0), (8, tok))
                rank = mm(needed.astype(BF16), earlier, NN)
                rank = jnp.where(needed > 0.0, rank, -1.0)[0:1, :]
                pick[which] = jnp.where(place == rank, 1.0, 0.0).astype(BF16)
        if index == 2:
            for copy in locals_[2:]:
                copy.wait()
            stage_one(0, tok)
        if index == 3:
            stage_two(0, 0, tok)
    for side in range(2):
        pack_last(side, 0)
    for part in range(2):
        for side in range(2):
            late(side, 0, part).wait_recv()
            late(side, 1, part).start()
    for side in range(2):
        packed_copy(side, 0).start()

    bufs = {"m": parts_m, "r": parts_r}
    orders = (RETURN_RIGHT, RETURN_LEFT)

    def back_copy(side, index):
        kind, step = orders[side][index]
        rows = few if index < 2 else tok
        return pltpu.make_async_remote_copy(
            src_ref=bufs[kind].at[pl.ds(slot_of(step) * tok, rows)],
            dst_ref=landed_few.at[side, index] if index < 2 else landed.at[side, index - 2],
            send_sem=rs_send.at[side, index], recv_sem=rs_recv.at[side, index],
            device_id={"expert": sides[side]}, device_id_type=MESH,
        )

    def return_first(index):
        for side in range(2):
            kind, step = orders[side][index]
            base = slot_of(step) * tok
            which = 0 if index == 0 else 2 - side
            squeeze(which, bufs[kind], base, bufs[kind].at[pl.ds(base, tok)])
            back_copy(side, index).start()

    def pair(j, carry):
        base = pl.multiple_of(j * 2 * tok, 2 * tok)

        @pl.when(j == 2)
        def _():
            for part in range(2):
                for side in range(2):
                    late(side, 1, part).wait_recv()
            for side in range(2):
                pack_last(side, 1)
                packed_copy(side, 1).start()

        @pl.when(j == 3)
        def _():
            for side in range(2):
                take_packed(side, 0)
            stage_one(tok, tok)
            stage_two(tok, tok, tok)
            return_first(0)
            for side in range(2):
                take_packed(side, 1)

        stage_one(base, 2 * tok)

        @pl.when(j < 3)
        def _():
            stage_two(base, base, 2 * tok)

        return carry

    lax.fori_loop(1, 4, pair, 0)
    stage_two(7 * tok, 6 * tok, tok)
    return_first(1)
    stage_two(6 * tok, 7 * tok, tok)

    lane = lax.broadcasted_iota(jnp.int32, (tok, 128), 1)
    stacked = jnp.zeros((tok, 128), F32)
    for slot in range(n):
        for e in range(exp_dev):
            stacked = jnp.where(lane == slot * 8 + e, dcol[e, pl.ds(slot * tok, tok), :], stacked)
    dsend[...] = jnp.transpose(stacked)[: n * 8].reshape(n, 8, 128)

    def dots_copy(slot):
        return pltpu.make_async_remote_copy(
            src_ref=dsend.at[slot], dst_ref=back.at[me],
            send_sem=small_send.at[1, slot], recv_sem=small_recv.at[1, slot],
            device_id={"expert": device_at(pos - step_of(slot))}, device_id_type=MESH,
        )

    for slot in range(1, n):
        dots_copy(slot).start()
    own_dots = pltpu.make_async_copy(dsend.at[0], back.at[me], local_sem.at[0])
    own_dots.start()

    def piece_rows(piece):
        return pl.ds(pl.multiple_of(piece * quarter, quarter), quarter)

    def weight_grads(piece):
        def tile(t, carry):
            base = pl.multiple_of(piece * quarter + t * 256, 256)
            for c in range(2):
                cols = pl.ds(c * exp_dev * ff, exp_dev * ff)
                dwgu[pl.ds(base, 256), cols] = mm(
                    x_all[:, pl.ds(base, 256)], dgu[:, cols], TN
                ).astype(BF16)
            return carry

        lax.fori_loop(0, quarter // 256, tile, 0)

    def down_grads(piece):
        def tile_down(t, carry):
            at = pl.multiple_of(t * 256, 256)
            dwd[piece, pl.ds(at, 256), :] = mm(
                mid[:, pl.ds(at, 256)], g_all[:, piece_rows(piece)], TN
            ).astype(BF16)
            return carry

        lax.fori_loop(0, exp_dev * ff // 256, tile_down, 0)

    def swap_copies(piece, where):
        return [
            pltpu.make_async_remote_copy(
                src_ref=src, dst_ref=dst, send_sem=dp_send.at[at], recv_sem=dp_recv.at[at],
                device_id={"dp": partner}, device_id_type=MESH,
            )
            for src, dst, at in (
                (dwgu.at[piece_rows(piece)], pr_gu.at[where], 2 * where),
                (dwd.at[piece], pr_d.at[where], 2 * where + 1),
            )
        ]

    far_own, far_partner = (1 - xpos) * 2 + core, (1 - xpos) * 2 + 1 - core
    near_own, near_partner = xpos * 2 + core, xpos * 2 + 1 - core
    far_swap = swap_copies(far_partner, 0)
    near_swap = swap_copies(near_partner, 1)
    far_send = [
        pltpu.make_async_remote_copy(
            src_ref=src, dst_ref=dst, send_sem=dp_send.at[at], recv_sem=dp_recv.at[at],
            device_id={"dp": across}, device_id_type=MESH,
        )
        for src, dst, at in (
            (dwgu.at[piece_rows(far_own)], xr_gu, 4),
            (dwd.at[far_own], xr_d, 5),
        )
    ]

    def return_step(index):
        for side in range(2):
            kind, step = orders[side][index]
            buf, base = bufs[kind], slot_of(step) * tok
            back_copy(side, index - 2).wait_recv()
            if index < 4:
                which = (5, 3)[side] if index == 2 else (6, 4)[side]

                def unpack(t, carry):
                    rows, cols = pl.ds(base, tok), pl.ds(pl.multiple_of(t * 512, 512), 512)
                    got = mm(pick[which], landed_few[side, index - 2, :, cols], TN)
                    buf[rows, cols] = (buf[rows, cols].astype(F32) + got).astype(BF16)
                    return carry

                lax.fori_loop(0, model // 512, unpack, 0)
                back_copy(side, index).start()
                continue

            def add(t, carry):
                rows = pl.ds(pl.multiple_of(base + t * 32, 32), 32)
                got = landed[side, index - 4, pl.ds(pl.multiple_of(t * 32, 32), 32), :]
                buf[rows, :] = (buf[rows, :].astype(F32) + got.astype(F32)).astype(BF16)
                return carry

            lax.fori_loop(0, tok // 32, add, 0)
            back_copy(side, index).start()

    weight_grads(far_partner)
    far_swap[0].start()
    return_step(2)
    weight_grads(far_own)
    far_swap[0].wait_recv()

    def add_far(t, carry):
        rows = pl.ds(pl.multiple_of(far_own * quarter + t * 32, 32), 32)
        got = pr_gu[0, pl.ds(pl.multiple_of(t * 32, 32), 32), :]
        dwgu[rows, :] = (dwgu[rows, :].astype(F32) + got.astype(F32)).astype(BF16)
        return carry

    lax.fori_loop(0, quarter // 32, add_far, 0)
    far_send[0].start()
    down_grads(far_partner)
    far_swap[1].start()
    down_grads(far_own)
    far_swap[1].wait_recv()

    def add_far_down(t, carry):
        rows = pl.ds(pl.multiple_of(t * 32, 32), 32)
        dwd[far_own, rows, :] = (
            dwd[far_own, rows, :].astype(F32) + pr_d[0, rows, :].astype(F32)
        ).astype(BF16)
        return carry

    lax.fori_loop(0, exp_dev * ff // 32, add_far_down, 0)
    far_send[1].start()
    return_step(3)
    weight_grads(near_partner)
    down_grads(near_partner)
    for copy in near_swap:
        copy.start()
    return_step(4)
    weight_grads(near_own)
    down_grads(near_own)
    return_step(5)

    own_dots.wait()
    for slot in range(1, n):
        dots_copy(slot).wait_recv()
    got = back[...].reshape(n * 8, tok)
    for k in range(top):
        dgates_ref[k : k + 1, :] = jnp.sum(
            jnp.where(ids_ref[k : k + 1, :] == expert_of_line, got, 0.0), axis=0, keepdims=True
        )
    return_step(6)

    for copy in near_swap:
        copy.wait_recv()
    far_send[0].wait_recv()

    def final_gu(t, carry):
        rows = pl.ds(pl.multiple_of(t * 32, 32), 32)
        own = pl.ds(pl.multiple_of(near_own * quarter + t * 32, 32), 32)
        total = (
            dwgu[own, :].astype(F32) + pr_gu[1, rows, :].astype(F32) + xr_gu[rows, :].astype(F32)
        ).astype(BF16)
        for e in range(exp_dev):
            sgate[e, rows, :] = total[:, e * ff : (e + 1) * ff]
            sup[e, rows, :] = total[:, (exp_dev + e) * ff : (exp_dev + e + 1) * ff]
        return carry

    def close_step(index):
        for side in range(2):
            back_copy(side, index).wait_recv()
        kind = orders[0][index][0]
        other = orders[1][index][0]
        for side, name in ((0, kind), (1, other)):
            buf, out = bufs[name], {"m": mixed_ref, "r": dtok_ref}[name]

            def close(t, carry):
                rows = pl.ds(pl.multiple_of(t * 32, 32), 32)
                so_far = buf if index == 5 else out
                out[rows, :] = (
                    so_far[rows, :].astype(F32) + landed[side, index - 2, rows, :].astype(F32)
                ).astype(BF16)
                return carry

            lax.fori_loop(0, tok // 32, close, 0)

    lax.fori_loop(0, quarter // 32, final_gu, 0)
    leaving = [
        pltpu.make_async_copy(sgate, ogate_ref, local_sem.at[1]),
        pltpu.make_async_copy(sup, oup_ref, local_sem.at[2]),
        pltpu.make_async_copy(sdown, odown_ref, local_sem.at[3]),
    ]
    leaving[0].start()
    leaving[1].start()
    close_step(5)
    far_send[1].wait_recv()
    for e in range(exp_dev):
        def final_down(t, carry):
            at = pl.multiple_of(t * 32, 32)
            rows = pl.ds(pl.multiple_of(e * ff + at, 32), 32)
            sdown[e, pl.ds(at, 32), :] = (
                dwd[near_own, rows, :].astype(F32)
                + pr_d[1, rows, :].astype(F32)
                + xr_d[rows, :].astype(F32)
            ).astype(BF16)
            return carry

        lax.fori_loop(0, ff // 32, final_down, 0)

    leaving[2].start()
    close_step(6)

    for side in range(2):
        for index in range(6):
            early(side, index).wait_send()
        for last in range(2):
            packed_copy(side, last).wait_send()
        for hop in range(2):
            for part in range(2):
                late(side, hop, part).wait_send()
        for index in range(7):
            back_copy(side, index).wait_send()
    for k in range(1, n):
        gate_copy(k).wait_send()
        dots_copy(k).wait_send()
    for case in range(4):
        relay_gates(case).wait_send()
    for copy in leaving:
        copy.wait()
    for copy in far_swap + near_swap + far_send:
        copy.wait_send()


def hand_over(*refs):
    held, sem = refs[12:18], refs[18]
    inward = [pltpu.make_async_copy(refs[i], held[i], sem.at[0, i]) for i in range(6)]
    outward = [pltpu.make_async_copy(held[i], refs[6 + i], sem.at[1, i]) for i in range(6)]
    for copy in inward:
        copy.start()
    for i in range(6):
        inward[i].wait()
        outward[i].start()
    for copy in outward:
        copy.wait()


def local(tokens, expert_ids, gate_weights, grad_out, w_gate, w_up, w_down):
    owners, dps = lax.axis_size("expert"), lax.axis_size("dp")
    if (owners, dps, *w_gate.shape[:1], tokens.shape[0]) != (8, 4, 2, 128):
        return local_wide(tokens, expert_ids, gate_weights, grad_out, w_gate, w_up, w_down)
    tok, model = tokens.shape
    exp_dev, _, ff = w_gate.shape
    rows, mids = owners * tok, exp_dev * ff
    quarter = model // dps
    few = exp_dev * CAP_DEV
    hbm = pl.BlockSpec(memory_space=pl.ANY)
    vmem = pl.BlockSpec(memory_space=pltpu.VMEM)
    dma = pltpu.SemaphoreType.DMA
    out = pl.pallas_call(
        layer_kernel,
        out_shape=(
            jax.ShapeDtypeStruct((tok, model), BF16),
            jax.ShapeDtypeStruct((tok, model), BF16),
            jax.ShapeDtypeStruct(gate_weights.shape[::-1], F32),
            jax.ShapeDtypeStruct((exp_dev, quarter, ff), BF16),
            jax.ShapeDtypeStruct((exp_dev, quarter, ff), BF16),
            jax.ShapeDtypeStruct((exp_dev, ff, quarter), BF16),
        ),
        in_specs=[hbm] * 5 + [vmem] * 2,
        out_specs=[vmem] * 3 + [hbm] * 3,
        scratch_shapes=[
            pltpu.VMEM((rows, model), BF16),
            pltpu.VMEM((rows, model), BF16),
            pltpu.VMEM((exp_dev, model, ff), BF16),
            pltpu.VMEM((exp_dev, model, ff), BF16),
            pltpu.VMEM((mids, model), BF16),
            pltpu.VMEM((rows, model), BF16),
            pltpu.VMEM((rows, model), BF16),
            pltpu.VMEM((rows, 2 * mids), BF16),
            pltpu.VMEM((rows, mids), BF16),
            pltpu.VMEM((model, 2 * mids), BF16),
            pltpu.VMEM((dps, mids, quarter), BF16),
            pltpu.VMEM((2, 5, tok, model), BF16),
            pltpu.VMEM((2, 2, few, model), BF16),
            pltpu.VMEM((2, quarter, 2 * mids), BF16),
            pltpu.VMEM((2, mids, quarter), BF16),
            pltpu.VMEM((quarter, 2 * mids), BF16),
            pltpu.VMEM((mids, quarter), BF16),
            pltpu.VMEM((owners, 8, 128), F32),
            pltpu.VMEM((owners + 4, 8, 128), F32),
            pltpu.VMEM((exp_dev, rows, 128), F32),
            pltpu.VMEM((exp_dev, rows, 128), F32),
            pltpu.VMEM((owners, 8, 128), F32),
            pltpu.VMEM((owners, 8, 128), F32),
            pltpu.VMEM((7, few, tok), BF16),
            pltpu.VMEM((2, 2, few, model), BF16),
            pltpu.VMEM((exp_dev, quarter, ff), BF16),
            pltpu.VMEM((exp_dev, quarter, ff), BF16),
            pltpu.VMEM((exp_dev, ff, quarter), BF16),
            dma((5,)),
            dma((2, 14)),
            dma((2, 14)),
            dma((2, 7)),
            dma((2, 7)),
            dma((2, 12)),
            dma((2, 12)),
            dma((6,)),
            dma((6,)),
        ],
        compiler_params=pltpu.CompilerParams(
            collective_id=0, has_side_effects=True, vmem_limit_bytes=67_043_328
        ),
        name="moe_layer",
    )(tokens, grad_out, w_gate, w_up, w_down.reshape(mids, model), expert_ids.T, gate_weights.T)
    out = pl.pallas_call(
        hand_over,
        out_shape=tuple(jax.ShapeDtypeStruct(v.shape, v.dtype) for v in out),
        in_specs=[hbm] * 6,
        out_specs=[hbm] * 6,
        scratch_shapes=[pltpu.VMEM(v.shape, v.dtype) for v in out] + [dma((2, 6))],
        compiler_params=pltpu.CompilerParams(vmem_limit_bytes=67_043_328),
        name="hand_over",
    )(*out)
    return (out[0], out[1], out[2].T, *out[3:])


def solution(mesh):
    in_specs = (
        P(("dp", "expert"), None),
        P(("dp", "expert"), None),
        P(("dp", "expert"), None),
        P(("dp", "expert"), None),
        P("expert", None, None),
        P("expert", None, None),
        P("expert", None, None),
    )
    out_specs = (
        P(("dp", "expert"), None),
        P(("dp", "expert"), None),
        P(("dp", "expert"), None),
        P("expert", "dp", None),
        P("expert", "dp", None),
        P("expert", None, "dp"),
    )
    return jax.shard_map(local, mesh=mesh, in_specs=in_specs, out_specs=out_specs, check_vma=False)
```
